32 devices in a mesh: fsdp: 4 (over y, x), seq: 8 (over z, core).
Axes of the slice: x: 2, y: 2, z: 4, core: 2. Of those that a mesh axis runs over, the one named last changes fastest.
Arguments:
- tokens: bfloat16 [8, 1024, 2048], P('fsdp', 'seq'), may hold values from -6 to 6
- positions: int32 [8, 1024], P('fsdp', 'seq'), may hold values from 0 to 2046, as said below
- gain_attn: bfloat16 [2048], P('fsdp'), may hold values from 0.099609375 to 1.8984375
- w_query: bfloat16 [2048, 2048], P('fsdp'), may hold values from -0.1875 to 0.1875
- w_key: bfloat16 [2048, 512], P('fsdp'), may hold values from -0.1875 to 0.1875
- w_value: bfloat16 [2048, 512], P('fsdp'), may hold values from -0.125 to 0.125
- w_out: bfloat16 [2048, 2048], P('fsdp'), may hold values from -0.5 to 0.5
- gain_ffn: bfloat16 [2048], P('fsdp'), may hold values from 0.099609375 to 1.8984375
- w_gate: bfloat16 [2048, 8192], P('fsdp'), may hold values from -0.125 to 0.125
- w_up: bfloat16 [2048, 8192], P('fsdp'), may hold values from -0.125 to 0.125
- w_down: bfloat16 [8192, 2048], P('fsdp'), may hold values from -0.0625 to 0.0625
- grad_out: bfloat16 [8, 1024, 2048], P('fsdp', 'seq'), may hold values from -6 to 6
Outputs:
- layer_out: bfloat16 [8, 1024, 2048], P('fsdp', 'seq')
- grad_tokens: bfloat16 [8, 1024, 2048], P('fsdp', 'seq')
- grad_gain_attn: float32 [2048], P('fsdp')
- grad_w_query: float32 [2048, 2048], P('fsdp')
- grad_w_key: float32 [2048, 512], P('fsdp')
- grad_w_value: float32 [2048, 512], P('fsdp')
- grad_w_out: float32 [2048, 2048], P('fsdp')
- grad_gain_ffn: float32 [2048], P('fsdp')
- grad_w_gate: float32 [2048, 8192], P('fsdp')
- grad_w_up: float32 [2048, 8192], P('fsdp')
- grad_w_down: float32 [8192, 2048], P('fsdp')
The draws below stay inside these ranges and needn't reach their ends.
Inputs may be any that keep to these rules, and one draw needn't show every extreme that they name: Along each sequence the positions rise strictly, by 1 or 2 from one token to the next.
All inputs are finite; a program needn't handle non-finite values.
Results may differ from the reference program's by a relative error of at most 0.02.
Values may be sent and summed in bfloat16 or wider, within the bound.
No kernel may reach another device: no remote copies, remote signals or barrier semaphores. Data moves between devices by JAX's collectives and lax.ppermute only.
A program may use at most 512 MiB of HBM per device.

```python
import math
import jax
import jax.numpy as jnp
from jax import lax

D = 2048
HEADS = 32
KV_HEADS = 8
HEAD_DIM = 64
FF = 8192
SEQS_DEV = 2
SEQ_LEN = 1024
BATCH = 8
KV_COPIES = 8
N_FSDP = 4


def draw_positions(key, part):
    step_sizes = jax.random.randint(key, (BATCH, SEQ_LEN), 1, 3, dtype=jnp.int32)
    rising = jnp.cumsum(step_sizes, axis=1, dtype=jnp.int32) - step_sizes[:, :1]
    top_place = 2 * SEQ_LEN - 2
    shift_up = top_place - rising[:, -1:]
    parity = (jnp.arange(BATCH, dtype=jnp.int32) % 2)[:, None]
    return rising + parity * shift_up


def steps_of(stream_key, extent, pieces, least, largest):
    def one(position, parts):
        steps = jax.random.uniform(jax.random.fold_in(jax.random.fold_in(stream_key, 6), position), (parts,), jnp.float32, least / len(pieces), largest / len(pieces))
        return jnp.repeat(jnp.exp(steps), extent[position] // parts).reshape((-1,) + (1,) * (len(extent) - position - 1))

    level = one(*pieces[0])
    for cut in pieces[1:]:
        level = level * one(*cut)
    return level


def scatter_about(stream_key, extent, scale, limit, pieces=(), held_as=jnp.bfloat16):
    values = scale * jax.random.normal(stream_key, extent, jnp.float32)
    if pieces:
        values = values * steps_of(stream_key, extent, pieces, -0.22, 0.18)
    return jnp.clip(values, -limit, limit).astype(held_as)


def setup_inputs(seed: int = 0) -> dict:
    streams_of = jax.random.split(jax.random.key(seed), 13)
    tokens = scatter_about(streams_of[0], (BATCH, SEQ_LEN, D), 1.0, 6.0, ((0, 4), (1, 8)))
    positions = draw_positions(jax.random.fold_in(streams_of[12], 71), 0)
    gain_attn = jnp.clip(1.0 + 0.18 * jax.random.normal(streams_of[2], (D,), jnp.float32), 0.099609375, 1.8984375).astype(jnp.bfloat16)
    w_query = scatter_about(streams_of[3], (D, HEADS * HEAD_DIM), (D // 2) ** -0.5, 0.1875, ((0, 4),))
    w_key = scatter_about(streams_of[4], (D, KV_HEADS * HEAD_DIM), (D // 2) ** -0.5, 0.1875, ((0, 4),))
    w_value = scatter_about(streams_of[5], (D, KV_HEADS * HEAD_DIM), D ** -0.5, 0.125, ((0, 4),))
    w_out = scatter_about(streams_of[6], (HEADS * HEAD_DIM, D), (HEADS * HEAD_DIM // 16) ** -0.5, 0.5, ((0, 4),))
    gain_ffn = jnp.clip(1.0 + 0.18 * jax.random.normal(streams_of[7], (D,), jnp.float32), 0.099609375, 1.8984375).astype(jnp.bfloat16)
    w_gate = scatter_about(streams_of[8], (D, FF), D ** -0.5, 0.125, ((0, 4),))
    w_up = scatter_about(streams_of[9], (D, FF), D ** -0.5, 0.125, ((0, 4),))
    w_down = scatter_about(streams_of[10], (FF, D), FF ** -0.5, 0.0625, ((0, 4),))
    grad_out = scatter_about(streams_of[11], (BATCH, SEQ_LEN, D), 1.0, 6.0, ((0, 4), (1, 8)))
    return {"tokens": tokens, "positions": positions, "gain_attn": gain_attn, "w_query": w_query, "w_key": w_key, "w_value": w_value, "w_out": w_out, "gain_ffn": gain_ffn, "w_gate": w_gate, "w_up": w_up, "w_down": w_down, "grad_out": grad_out}


@jax.custom_vjp
def low(v):
    return lax.optimization_barrier(v.astype(jnp.bfloat16)).astype(jnp.float32)

@jax.custom_vjp
def low_back(v):
    return v

def low_keep(v):
    return (low(v), None)

def low_pass(kept, grad):
    return (grad,)

def back_keep(v):
    return (v, None)

def back_low(kept, grad):
    return (low(grad),)
low.defvjp(low_keep, low_pass)
low_back.defvjp(back_keep, back_low)
norm_eps = 1e-05
theta_log = math.log(500000.0)

def rope_tables(places, half_dim):
    freqs = jnp.exp(jnp.arange(half_dim, dtype=jnp.float32) * (-2.0 * theta_log / (2 * half_dim)))
    angles = places.astype(jnp.float32)[..., None] * freqs
    return (jnp.cos(angles), jnp.sin(angles))

def rotate(field, cos_tab, sin_tab):
    half_dim = field.shape[-1] // 2
    lower_half = field[..., :half_dim]
    upper_half = field[..., half_dim:]
    return jnp.concatenate([lower_half * cos_tab - upper_half * sin_tab, upper_half * cos_tab + lower_half * sin_tab], -1)

def matmul(inputs, weight):
    return jnp.einsum('gtd,df->gtf', inputs, weight, precision=lax.Precision.HIGHEST)

def forward(hidden_in, places, gain_a, wq_f, wk_f, wv_f, wo_f, gain_f, wg_f, wu_f, wd_f):
    groups_n, seq_len, _ = hidden_in.shape
    inv_one = lax.rsqrt(lax.optimization_barrier(jnp.mean(hidden_in * hidden_in, -1, keepdims=True)) + norm_eps)
    normed_one = low(hidden_in * inv_one * gain_a)
    query = low_back(matmul(normed_one, wq_f)).reshape(groups_n, seq_len, HEADS, HEAD_DIM)
    key_raw = low_back(matmul(normed_one, wk_f)).reshape(groups_n, seq_len, KV_HEADS, HEAD_DIM)
    value_raw = low_back(matmul(normed_one, wv_f)).reshape(groups_n, seq_len, KV_HEADS, HEAD_DIM)
    cos_tab, sin_tab = rope_tables(places, HEAD_DIM // 2)
    cos_tab = cos_tab[:, :, None, :]
    sin_tab = sin_tab[:, :, None, :]
    q_rot = low(low_back(rotate(query, cos_tab, sin_tab)))
    k_rot = low(rotate(key_raw, cos_tab, sin_tab))
    v_low = low(value_raw)
    repeats = KV_COPIES // KV_HEADS
    k_copy = low_back(jnp.repeat(k_rot, repeats, axis=2))
    v_copy = low_back(jnp.repeat(v_low, repeats, axis=2))
    per_copy = HEADS // KV_COPIES
    k_heads = jnp.repeat(k_copy, per_copy, axis=2)
    v_heads = jnp.repeat(v_copy, per_copy, axis=2)
    block_len = min(512, seq_len)
    n_blocks = seq_len // block_len
    logit_scale = HEAD_DIM ** (-0.5)

    def one_block(block_idx):
        offset = block_idx * block_len
        q_block = lax.dynamic_slice_in_dim(q_rot, offset, block_len, 1)
        q_places = lax.dynamic_slice_in_dim(places, offset, block_len, 1)
        raw_logits = jnp.einsum('gqhd,gkhd->ghqk', q_block, k_heads, precision=lax.Precision.HIGHEST) * logit_scale
        allowed = places[:, None, None, :] <= q_places[:, None, :, None]
        logits = jnp.where(allowed, low_back(raw_logits), -1e+30)
        row_max = lax.optimization_barrier(jnp.max(logits, -1, keepdims=True))
        weights_exp = jnp.exp(logits - row_max)
        prob_low = low(weights_exp / lax.optimization_barrier(jnp.sum(weights_exp, -1, keepdims=True)))
        return jnp.einsum('ghqk,gkhd->gqhd', prob_low, v_heads, precision=lax.Precision.HIGHEST)
    checked = jax.checkpoint(one_block)
    blocks_out = lax.map(checked, jnp.arange(n_blocks, dtype=jnp.int32))
    attended = jnp.moveaxis(blocks_out, 0, 1).reshape(groups_n, seq_len, HEADS * HEAD_DIM)
    attended = low(low_back(attended))
    resid = hidden_in + low_back(matmul(attended, wo_f))
    inv_two = lax.rsqrt(lax.optimization_barrier(jnp.mean(resid * resid, -1, keepdims=True)) + norm_eps)
    normed_two = low(resid * inv_two * gain_f)
    gate = low_back(matmul(normed_two, wg_f))
    upper = low_back(matmul(normed_two, wu_f))
    hidden = low(gate * jax.nn.sigmoid(gate) * upper)
    return resid + matmul(hidden, wd_f)

def reference(tokens, positions, gain_attn, w_query, w_key, w_value, w_out, gain_ffn, w_gate, w_up, w_down, grad_out):
    params = tuple((weight.astype(jnp.float32) for weight in (gain_attn, w_query, w_key, w_value, w_out, gain_ffn, w_gate, w_up, w_down)))
    tok_groups = tokens.astype(jnp.float32).reshape(N_FSDP, SEQS_DEV, SEQ_LEN, D)
    place_groups = positions.reshape(N_FSDP, SEQS_DEV, SEQ_LEN)
    cot_groups = grad_out.astype(jnp.float32).reshape(N_FSDP, SEQS_DEV, SEQ_LEN, D)
    zeros_acc = tuple((jnp.zeros_like(weight) for weight in params))

    def group_step(accum, item):
        tok_group, place_group, cot_group = item

        def closed(hidden_in, *weights):
            return forward(hidden_in, place_group, *weights)
        result, pullback = jax.vjp(closed, tok_group, *params)
        grads = pullback(cot_group)
        accum = tuple((total + grad for total, grad in zip(accum, grads[1:])))
        return (accum, (result.astype(jnp.bfloat16), grads[0].astype(jnp.bfloat16)))
    accum, (outputs, input_grads) = lax.scan(group_step, zeros_acc, (tok_groups, place_groups, cot_groups))
    layer_out = outputs.reshape(BATCH, SEQ_LEN, D)
    grad_tokens = input_grads.reshape(BATCH, SEQ_LEN, D)
    return (layer_out, grad_tokens, accum[0], accum[1], accum[2], accum[3], accum[4], accum[5], accum[6], accum[7], accum[8])
```

```python
import functools
import math

import jax
import jax.numpy as jnp
import numpy as np
from jax import lax
from jax.experimental import pallas as pl
from jax.experimental.pallas import tpu as pltpu
from jax.sharding import Mesh
from jax.sharding import PartitionSpec as P

HEADS = 32
KV_HEADS = 8
HEAD_DIM = 64
GROUP = HEADS // KV_HEADS
LANES = 128

norm_eps = 1e-05
theta_log = math.log(500000.0)
BF = jnp.bfloat16
F32 = jnp.float32


def xor_send(field, bit):
    count = lax.axis_size("fsdp")
    return lax.ppermute(field, "fsdp", [(i, i ^ bit) for i in range(count)])


def core_swap(field):
    return lax.ppermute(field, "core", [(0, 1), (1, 0)])


def gather_rel(own):
    count = lax.axis_size("fsdp")
    if count == 4:
        half = own.shape[0] // 2
        one = xor_send(own, 1)
        two = xor_send(own, 2)
        top = xor_send(one[:half], 2)
        low = xor_send(two[half:], 1)
        return [own, one, two, jnp.concatenate([top, low], 0)]
    chunks = [own]
    bit = 1
    while bit < count:
        chunks = chunks + [xor_send(chunk, bit) for chunk in chunks]
        bit *= 2
    return chunks


def reduce_rel(partials):
    count = lax.axis_size("fsdp")
    if count == 4:
        zero, one, two, three = partials
        half = three.shape[0] // 2
        top = xor_send(three[:half], 1)
        low = xor_send(three[half:], 2)
        two = jnp.concatenate([add_low(two[:half], top), two[half:]], 0)
        one = jnp.concatenate([one[:half], add_low(one[half:], low)], 0)
        one = xor_send(one, 1)
        two = xor_send(two, 2)
        return zero.astype(F32) + one.astype(F32) + two.astype(F32)
    chunks = list(partials)
    bit = count // 2
    while bit >= 1:
        sent = [xor_send(chunks[bit + i].astype(BF), bit) for i in range(bit)]
        chunks = [chunks[i].astype(F32) + sent[i].astype(F32) for i in range(bit)]
        bit //= 2
    return chunks[0]


def add_low(left, right):
    return (left.astype(F32) + right.astype(F32)).astype(BF)


def z_steps():
    count = lax.axis_size("zed")
    half = count // 2
    inwards = [[(i, i + 1), (count - 1 - i, count - 2 - i)] for i in range(half - 1)]
    outwards = [[(b, a) for a, b in pairs] for pairs in reversed(inwards)]
    middle = [(half - 1, half), (half, half - 1)]
    return [(pairs, True) for pairs in inwards + [middle]] + [(pairs, False) for pairs in outwards]


def z_move(field, stage):
    return lax.ppermute(field, "zed", z_steps()[stage][0])


def z_join(field, moved, stage):
    pairs, adds = z_steps()[stage]
    if adds:
        return add_low(field, moved)
    place = lax.axis_index("zed")
    return jnp.where((place == pairs[0][1]) | (place == pairs[1][1]), moved, field)


class Line:
    def __init__(self):
        self.last = len(z_steps())
        self.running = []
        self.ready = {}

    def round(self, tie, **fields):
        self.running += [(name, 0, field) for name, field in fields.items()]
        moved = [z_move(field, stage) for _, stage, field in self.running]
        tie, moved = lax.optimization_barrier((tie, moved))
        left = []
        for (name, stage, field), arrived in zip(self.running, moved):
            field = z_join(field, arrived, stage)
            if stage + 1 == self.last:
                self.ready[name] = field
            else:
                left.append((name, stage + 1, field))
        self.running = left
        return tie

    def take(self, *names):
        while not all(name in self.ready for name in names):
            self.round(())
        return [self.ready[name] for name in names]

    def hold(self, tie):
        held = [field for _, _, field in self.running]
        tie, held = lax.optimization_barrier((tie, held))
        self.running = [(name, stage, h) for (name, stage, _), h in zip(self.running, held)]
        return tie


def z_up(field):
    count = lax.axis_size("zed")
    return lax.ppermute(field, "zed", [(i, i + 1) for i in range(count - 1)])


def z_down(field):
    count = lax.axis_size("zed")
    return lax.ppermute(field, "zed", [(i + 1, i) for i in range(count - 1)])


def cost(flops, transcendentals, bytes_accessed):
    return pl.CostEstimate(
        flops=flops // 4, transcendentals=transcendentals // 4, bytes_accessed=bytes_accessed // 4
    )


def rotated(field, cos_tab, sin_tab):
    lane = lax.broadcasted_iota(jnp.int32, field.shape, 1)
    other = jnp.where(
        lane % HEAD_DIM < HEAD_DIM // 2,
        pltpu.roll(field, LANES - HEAD_DIM // 2, 1),
        pltpu.roll(field, HEAD_DIM // 2, 1),
    )
    return field * cos_tab + other * sin_tab


def kv_tables(cos_tab, sin_tab):
    lane = lax.broadcasted_iota(jnp.int32, cos_tab.shape, 1)
    return (
        jnp.where(lane < HEAD_DIM, cos_tab, 1.0),
        jnp.where(lane < HEAD_DIM, sin_tab, 0.0),
    )


def block_lanes(i, core, shard):
    half = shard // 2
    return pl.ds(pl.multiple_of(i * shard + core * half, half), half)


def project_kernel(
    place_ref, x_ref, gain_ref, own_ref, other_ref, cos_ref, sin_ref, h_ref, q_ref, kv_ref
):
    x = x_ref[...].astype(F32)
    inv = lax.rsqrt(jnp.mean(x * x, -1, keepdims=True) + norm_eps)
    h_ref[...] = (x * inv * gain_ref[...]).astype(BF)
    cos_tab = cos_ref[...]
    sin_tab = sin_ref[...]
    kv_cos, kv_sin = kv_tables(cos_tab, sin_tab)
    core = place_ref[1]
    raw = jnp.zeros((x.shape[0], own_ref.shape[2]), F32)
    for i in range(own_ref.shape[0]):
        for ref, side in ((own_ref, core), (other_ref, 1 - core)):
            cols = block_lanes(i, side, 2 * own_ref.shape[1])
            raw = raw + jnp.dot(h_ref[:, cols], ref[i], preferred_element_type=F32)
    q_width = q_ref.shape[1]
    for start in range(0, q_width, LANES):
        part = rotated(raw[:, start : start + LANES], cos_tab, sin_tab)
        q_ref[:, start : start + LANES] = (part * HEAD_DIM**-0.5).astype(BF)
    for start in range(0, kv_ref.shape[1], LANES):
        part = rotated(raw[:, q_width + start : q_width + start + LANES], kv_cos, kv_sin)
        kv_ref[:, start : start + LANES] = part.astype(BF)


def project(place, x, gain, w_own, w_other, cos_tab, sin_tab, kv_width):
    rows, width = x.shape
    all_width = w_own.shape[2]
    q_width = all_width - kv_width
    return pl.pallas_call(
        project_kernel,
        in_specs=[pl.BlockSpec(memory_space=pltpu.SMEM)]
        + [pl.BlockSpec(memory_space=pltpu.VMEM)] * 6,
        out_shape=(
            jax.ShapeDtypeStruct((rows, width), BF),
            jax.ShapeDtypeStruct((rows, q_width), BF),
            jax.ShapeDtypeStruct((rows, kv_width), BF),
        ),
        compiler_params=pltpu.CompilerParams(vmem_limit_bytes=40 << 20),
        cost_estimate=cost(
            flops=2 * rows * width * all_width,
            transcendentals=rows,
            bytes_accessed=4 * rows * width + 2 * width * all_width,
        ),
        name="project",
    )(place, x, gain, w_own, w_other, cos_tab, sin_tab)


def unrotate_kernel(dq_ref, cos_ref, sin_ref, d_ref):
    for start in range(0, dq_ref.shape[1], LANES):
        part = dq_ref[:, start : start + LANES].astype(F32)
        d_ref[:, start : start + LANES] = rotated(part, cos_ref[...], -sin_ref[...]).astype(BF)


def unrotate(dq, cos_tab, sin_tab, block):
    rows, wide = dq.shape
    tables = pl.BlockSpec((block, LANES), lambda i: (i, 0))
    field = pl.BlockSpec((block, wide), lambda i: (i, 0))
    return pl.pallas_call(
        unrotate_kernel,
        grid=(rows // block,),
        in_specs=[field, tables, tables],
        out_specs=field,
        out_shape=jax.ShapeDtypeStruct(dq.shape, BF),
        cost_estimate=cost(
            flops=6 * rows * wide, transcendentals=0, bytes_accessed=6 * rows * wide
        ),
        name="unrotate",
    )(dq, cos_tab, sin_tab)


def unproject_kernel(
    place_ref, dq_ref, dkv_ref, own_ref, other_ref, cos_ref, sin_ref, d_ref, dh_ref
):
    kv_cos, kv_sin = kv_tables(cos_ref[...], -sin_ref[...])
    q_width = dq_ref.shape[1]
    for start in range(0, dkv_ref.shape[1], LANES):
        part = rotated(dkv_ref[:, start : start + LANES].astype(F32), kv_cos, kv_sin)
        d_ref[:, start : start + LANES] = part.astype(BF)
    core = place_ref[1]
    across = (((1,), (1,)), ((), ()))
    for i in range(own_ref.shape[0]):
        for ref, side in ((own_ref, core), (other_ref, 1 - core)):
            cols = block_lanes(i, side, 2 * own_ref.shape[1])
            total = lax.dot_general(
                dq_ref[...], ref[i, :, :q_width], across, preferred_element_type=F32
            )
            total = total + lax.dot_general(
                d_ref[...], ref[i, :, q_width:], across, preferred_element_type=F32
            )
            dh_ref[:, cols] = total.astype(BF)


def unproject(place, dq, dkv, w_own, w_other, cos_tab, sin_tab):
    rows = dq.shape[0]
    count, half, cols = w_own.shape
    width = 2 * count * half
    block = rows // count

    def row_block(wide):
        return pl.BlockSpec((block, wide), lambda i, place: (i, 0))

    weights = pl.BlockSpec(w_own.shape, lambda i, place: (0, 0, 0))
    return pl.pallas_call(
        unproject_kernel,
        grid_spec=pltpu.PrefetchScalarGridSpec(
            num_scalar_prefetch=1,
            grid=(rows // block,),
            in_specs=[
                row_block(dq.shape[1]),
                row_block(dkv.shape[1]),
                weights,
                weights,
                row_block(LANES),
                row_block(LANES),
            ],
            out_specs=(row_block(dkv.shape[1]), row_block(width)),
        ),
        out_shape=(
            jax.ShapeDtypeStruct(dkv.shape, BF),
            jax.ShapeDtypeStruct((rows, width), BF),
        ),
        compiler_params=pltpu.CompilerParams(vmem_limit_bytes=40 << 20),
        cost_estimate=cost(
            flops=2 * rows * width * cols,
            transcendentals=0,
            bytes_accessed=2 * rows * width + 2 * width * cols + 4 * rows * cols,
        ),
        name="unproject",
    )(place, dq, dkv, w_own, w_other, cos_tab, sin_tab)


def pick_units(place, w_even, w_odd, count):
    high, wide = w_even.shape
    units = wide // count // 2

    def kernel(place_ref, even_ref, odd_ref, out_ref):
        even = place_ref[0] % 2 == 0

        @pl.when(even)
        def _():
            out_ref[0] = even_ref[...]

        @pl.when(jnp.logical_not(even))
        def _():
            out_ref[0] = odd_ref[...]

    def columns(parity):
        def index(i, place):
            here = place[0] % 2 == parity
            return (0, jnp.where(here, 2 * i + place[1], 0))

        return pl.BlockSpec((high, units), index)

    return pl.pallas_call(
        kernel,
        grid_spec=pltpu.PrefetchScalarGridSpec(
            num_scalar_prefetch=1,
            grid=(count,),
            in_specs=[columns(0), columns(1)],
            out_specs=pl.BlockSpec((1, high, units), lambda i, place: (i, 0, 0)),
        ),
        out_shape=jax.ShapeDtypeStruct((count, high, units), BF),
        cost_estimate=cost(
            flops=0, transcendentals=0, bytes_accessed=4 * count * high * units
        ),
        name="pick_units",
    )(place, w_even, w_odd)


def pick_heads(place, w_query, w_key, w_value, count):
    high = w_query.shape[0] // 2
    q_width = w_query.shape[1] // count
    k_width = w_key.shape[1] // count

    def kernel(place_ref, q_ref, k_ref, v_ref, out_ref):
        for i in range(count):
            out_ref[i, :, :q_width] = q_ref[:, i * q_width : (i + 1) * q_width]
            for head in range(k_width // HEAD_DIM):
                cols = slice(i * k_width + head * HEAD_DIM, i * k_width + (head + 1) * HEAD_DIM)
                start = q_width + head * LANES
                out_ref[i, :, start : start + LANES] = jnp.concatenate(
                    [k_ref[:, cols], v_ref[:, cols]], 1
                )

    def half(weight):
        return pl.BlockSpec((high, weight.shape[1]), lambda i, place: (place[1], 0))

    all_width = q_width + 2 * k_width
    return pl.pallas_call(
        kernel,
        grid_spec=pltpu.PrefetchScalarGridSpec(
            num_scalar_prefetch=1,
            grid=(1,),
            in_specs=[half(w_query), half(w_key), half(w_value)],
            out_specs=pl.BlockSpec((count, high, all_width), lambda i, place: (0, 0, 0)),
        ),
        out_shape=jax.ShapeDtypeStruct((count, high, all_width), BF),
        cost_estimate=cost(
            flops=0, transcendentals=0, bytes_accessed=4 * count * high * all_width
        ),
        name="pick_heads",
    )(place, w_query, w_key, w_value)


def feed_kernel(place_ref, h_ref, cot_ref, w0_ref, w1_ref, wd_ref, hidden_ref, dg_ref, du_ref):
    high = h_ref.shape[0] // 2

    def run(wg_ref, wu_ref):
        for start in (0, high):
            rows = slice(start, start + high)
            gate = jnp.dot(h_ref[rows], wg_ref[...], preferred_element_type=F32)
            upper = jnp.dot(h_ref[rows], wu_ref[...], preferred_element_type=F32)
            gate_sig = jax.nn.sigmoid(gate)
            gate_act = gate * gate_sig
            hidden_ref[rows] = (gate_act * upper).astype(BF)
            d_hidden = lax.dot_general(
                cot_ref[rows], wd_ref[...], (((1,), (1,)), ((), ())), preferred_element_type=F32
            )
            d_gate = d_hidden * upper * (gate_sig + gate_act * (1.0 - gate_sig))
            dg_ref[rows] = d_gate.astype(BF)
            du_ref[rows] = (d_hidden * gate_act).astype(BF)

    even = place_ref[0] % 2 == 0

    @pl.when(even)
    def _():
        run(w0_ref, w1_ref)

    @pl.when(jnp.logical_not(even))
    def _():
        run(w1_ref, w0_ref)


def feed(place, h_all, cot_all, w0, w1, w_down, side):
    rows, width = h_all.shape
    units = w0.shape[1]
    block = min(256, units)
    steps = units // block
    full = pl.BlockSpec((rows, width), lambda j, place: (0, 0))
    columns = pl.BlockSpec((width, block), lambda j, place: (0, j))
    out = pl.BlockSpec((rows, block), lambda j, place: (0, j))
    return pl.pallas_call(
        feed_kernel,
        grid_spec=pltpu.PrefetchScalarGridSpec(
            num_scalar_prefetch=1,
            grid=(steps,),
            in_specs=[
                full,
                full,
                columns,
                columns,
                pl.BlockSpec(
                    (block, width), lambda j, place: ((place[1] + side) % 2 * steps + j, 0)
                ),
            ],
            out_specs=[out] * 3,
        ),
        out_shape=[jax.ShapeDtypeStruct((rows, units), BF)] * 3,
        compiler_params=pltpu.CompilerParams(vmem_limit_bytes=56 << 20),
        cost_estimate=cost(
            flops=6 * rows * width * units,
            transcendentals=rows * units,
            bytes_accessed=4 * rows * width + 6 * width * units + 6 * rows * units,
        ),
        name="feed",
    )(place, h_all, cot_all, w0, w1, w_down)


def unfeed(place, dg, du, w0, w1, first, last):
    high = last - first
    units = dg[0].shape[1]
    width = w0[0].shape[0]
    block = min(512, width)
    across = (((1,), (1,)), ((), ()))

    def kernel(place_ref, dg0, dg1, du0, du1, w00, w01, w10, w11, out_ref):
        def run(*pairs):
            total = None
            for d_ref, w_ref in pairs:
                part = lax.dot_general(
                    d_ref[...], w_ref[...], across, preferred_element_type=F32
                )
                total = part if total is None else total + part
            out_ref[...] = total.astype(BF)

        even = place_ref[0] % 2 == 0

        @pl.when(even)
        def _():
            run((dg0, w00), (du0, w10), (dg1, w01), (du1, w11))

        @pl.when(jnp.logical_not(even))
        def _():
            run((du0, w00), (dg0, w10), (du1, w01), (dg1, w11))

    return pl.pallas_call(
        kernel,
        grid_spec=pltpu.PrefetchScalarGridSpec(
            num_scalar_prefetch=1,
            grid=(width // block,),
            in_specs=[pl.BlockSpec((high, units), lambda n, place: (first // high, 0))] * 4
            + [pl.BlockSpec((block, units), lambda n, place: (n, 0))] * 4,
            out_specs=pl.BlockSpec((high, block), lambda n, place: (0, n)),
        ),
        out_shape=jax.ShapeDtypeStruct((high, width), BF),
        compiler_params=pltpu.CompilerParams(vmem_limit_bytes=48 << 20),
        cost_estimate=cost(
            flops=8 * high * units * width,
            transcendentals=0,
            bytes_accessed=8 * width * units + 8 * high * units + 2 * high * width,
        ),
        name="unfeed",
    )(place, *dg, *du, *w0, *w1)


def lower(place, hidden, w_down):
    rows, units = hidden[0].shape
    width = w_down.shape[1]
    block = min(512, width)

    def kernel(place_ref, h0, h1, w0, w1, out_ref):
        total = jnp.dot(h0[...], w0[...], preferred_element_type=F32)
        total = total + jnp.dot(h1[...], w1[...], preferred_element_type=F32)
        out_ref[...] = total.astype(BF)

    return pl.pallas_call(
        kernel,
        grid_spec=pltpu.PrefetchScalarGridSpec(
            num_scalar_prefetch=1,
            grid=(width // block,),
            in_specs=[pl.BlockSpec((rows, units), lambda n, place: (0, 0))] * 2
            + [
                pl.BlockSpec((units, block), lambda n, place: (place[1], n)),
                pl.BlockSpec((units, block), lambda n, place: (1 - place[1], n)),
            ],
            out_specs=pl.BlockSpec((rows, block), lambda n, place: (0, n)),
        ),
        out_shape=jax.ShapeDtypeStruct((rows, width), BF),
        compiler_params=pltpu.CompilerParams(vmem_limit_bytes=48 << 20),
        cost_estimate=cost(
            flops=4 * rows * units * width,
            transcendentals=0,
            bytes_accessed=4 * width * units + 4 * rows * units + 2 * rows * width,
        ),
        name="lower",
    )(place, *hidden, w_down, w_down)


def low_lanes(shape):
    return lax.broadcasted_iota(jnp.int32, shape, 1) < HEAD_DIM


def stack_heads(ref, group, upper):
    rows = []
    for head in range(0, GROUP, 2):
        start = (group * GROUP + head) * HEAD_DIM
        pair = ref[:, start : start + LANES].astype(F32)
        turned = pltpu.roll(pair, HEAD_DIM, 1)
        keep = low_lanes(pair.shape)
        if upper:
            keep = jnp.logical_not(keep)
            rows += [jnp.where(keep, turned, 0.0), jnp.where(keep, pair, 0.0)]
        else:
            rows += [jnp.where(keep, pair, 0.0), jnp.where(keep, turned, 0.0)]
    return jnp.concatenate(rows, 0).astype(BF)


def unstack_heads(stacked, ref, group, upper):
    span = ref.shape[0]
    for head in range(0, GROUP, 2):
        even = stacked[head * span : (head + 1) * span]
        odd = stacked[(head + 1) * span : (head + 2) * span]
        keep = low_lanes(even.shape)
        if upper:
            pair = jnp.where(keep, pltpu.roll(even, HEAD_DIM, 1), odd)
        else:
            pair = jnp.where(keep, even, pltpu.roll(odd, HEAD_DIM, 1))
        start = (group * GROUP + head) * HEAD_DIM
        ref[:, start : start + LANES] = pair.astype(ref.dtype)


def logits_of(place_ref, q_all, kv_own, kv_rest, span):
    own = lax.dot_general(q_all, kv_own, (((1,), (1,)), ((), ())), preferred_element_type=F32)
    rest = lax.dot_general(q_all, kv_rest, (((1,), (1,)), ((), ())), preferred_element_type=F32)
    row = lax.broadcasted_iota(jnp.int32, own.shape, 0) % span
    col = lax.broadcasted_iota(jnp.int32, own.shape, 1)
    own = jnp.where(col <= row, own, -1e30)
    block = lax.broadcasted_iota(jnp.int32, (1, rest.shape[1]), 1) // span + 1
    have = jnp.where(block == 1, place_ref[1], place_ref[0])
    need = jnp.where(block == 1, 1, block // 2)
    rest = rest + jnp.where(have >= need, 0.0, -1e30)
    return own, rest


def attend_kernel(place_ref, q_ref, *refs):
    kv_refs = refs[:-2]
    out_ref, lse_ref = refs[-2:]
    span = q_ref.shape[0]
    for group in range(lse_ref.shape[1]):
        cols = slice(group * LANES, (group + 1) * LANES)
        q_all = stack_heads(q_ref, group, False)
        kv_own = kv_refs[0][:, cols]
        kv_rest = jnp.concatenate([ref[:, cols] for ref in kv_refs[1:]], 0)
        own, rest = logits_of(place_ref, q_all, kv_own, kv_rest, span)
        top = jnp.maximum(jnp.max(own, -1, keepdims=True), jnp.max(rest, -1, keepdims=True))
        own = jnp.exp(own - top)
        rest = jnp.exp(rest - top)
        total = jnp.sum(own, -1, keepdims=True) + jnp.sum(rest, -1, keepdims=True)
        out = jnp.dot(own.astype(BF), kv_own, preferred_element_type=F32)
        out = out + jnp.dot(rest.astype(BF), kv_rest, preferred_element_type=F32)
        unstack_heads(out / total, out_ref, group, True)
        lse_ref[0, group] = top + jnp.log(total)


def attend_back_kernel(place_ref, q_ref, do_ref, lse_ref, *refs):
    count = (len(refs) - 1) // 2
    kv_refs = refs[:count]
    dq_ref = refs[count]
    dkv_refs = refs[count + 1 :]
    span = q_ref.shape[0]
    flip = (((0,), (0,)), ((), ()))
    across = (((1,), (1,)), ((), ()))
    for group in range(lse_ref.shape[1]):
        cols = slice(group * LANES, (group + 1) * LANES)
        q_all = stack_heads(q_ref, group, False)
        do_all = stack_heads(do_ref, group, True)
        kv_own = kv_refs[0][:, cols]
        kv_rest = jnp.concatenate([ref[:, cols] for ref in kv_refs[1:]], 0)
        own, rest = logits_of(place_ref, q_all, kv_own, kv_rest, span)
        lse = lse_ref[0, group]
        own = jnp.exp(own - lse)
        rest = jnp.exp(rest - lse)
        d_own = lax.dot_general(do_all, kv_own, across, preferred_element_type=F32)
        d_rest = lax.dot_general(do_all, kv_rest, across, preferred_element_type=F32)
        inner = jnp.sum(own * d_own, -1, keepdims=True) + jnp.sum(rest * d_rest, -1, keepdims=True)
        d_own = (own * (d_own - inner)).astype(BF)
        d_rest = (rest * (d_rest - inner)).astype(BF)
        dq = jnp.dot(d_own, kv_own, preferred_element_type=F32)
        dq = dq + jnp.dot(d_rest, kv_rest, preferred_element_type=F32)
        unstack_heads(dq * HEAD_DIM**-0.5, dq_ref, group, False)
        dkv = lax.dot_general(d_own, q_all, flip, preferred_element_type=F32)
        dkv = dkv + lax.dot_general(own.astype(BF), do_all, flip, preferred_element_type=F32)
        dkv_refs[0][:, cols] = dkv.astype(BF)
        dkv = lax.dot_general(d_rest, q_all, flip, preferred_element_type=F32)
        dkv = dkv + lax.dot_general(rest.astype(BF), do_all, flip, preferred_element_type=F32)
        for i, ref in enumerate(dkv_refs[1:]):
            ref[:, cols] = dkv[i * span : (i + 1) * span].astype(BF)


def attend_specs(q_all, kv_all, span):
    kv_width = kv_all[0].shape[1]
    groups = kv_width // LANES
    return (
        pl.BlockSpec((span, q_all.shape[1]), lambda i, place: (i, 0)),
        pl.BlockSpec((span, kv_width), lambda i, place: (i, 0)),
        pl.BlockSpec((1, groups, GROUP * span, 1), lambda i, place: (i, 0, 0, 0)),
        groups,
    )


def attend(place, q_all, kv_all, span):
    rows = q_all.shape[0]
    q_spec, kv_spec, lse_spec, groups = attend_specs(q_all, kv_all, span)
    cells = rows * groups * GROUP * span * len(kv_all)
    return pl.pallas_call(
        attend_kernel,
        grid_spec=pltpu.PrefetchScalarGridSpec(
            num_scalar_prefetch=1,
            grid=(rows // span,),
            in_specs=[q_spec] + [kv_spec] * len(kv_all),
            out_specs=[q_spec, lse_spec],
        ),
        out_shape=(
            jax.ShapeDtypeStruct(q_all.shape, BF),
            jax.ShapeDtypeStruct((rows // span, groups, GROUP * span, 1), F32),
        ),
        compiler_params=pltpu.CompilerParams(vmem_limit_bytes=56 << 20),
        cost_estimate=cost(
            flops=2 * 4 * LANES * cells, transcendentals=cells, bytes_accessed=16 << 20
        ),
        name="attend",
    )(place, q_all, *kv_all)


def attend_back(place, q_all, do_all, lse, kv_all, span):
    rows = q_all.shape[0]
    q_spec, kv_spec, lse_spec, groups = attend_specs(q_all, kv_all, span)
    cells = rows * groups * GROUP * span * len(kv_all)
    outs = pl.pallas_call(
        attend_back_kernel,
        grid_spec=pltpu.PrefetchScalarGridSpec(
            num_scalar_prefetch=1,
            grid=(rows // span,),
            in_specs=[q_spec, q_spec, lse_spec] + [kv_spec] * len(kv_all),
            out_specs=[q_spec] + [kv_spec] * len(kv_all),
        ),
        out_shape=[jax.ShapeDtypeStruct(q_all.shape, BF)]
        + [jax.ShapeDtypeStruct(kv.shape, BF) for kv in kv_all],
        compiler_params=pltpu.CompilerParams(vmem_limit_bytes=60 << 20),
        cost_estimate=cost(
            flops=2 * 8 * LANES * cells, transcendentals=cells, bytes_accessed=24 << 20
        ),
        name="attend_back",
    )(place, q_all, do_all, lse, *kv_all)
    return outs[0], outs[1:]


def spread_kernel(place_ref, own_ref, other_ref, out_ref):
    @pl.when(pl.program_id(1) == 0)
    def _():
        out_ref[...] = own_ref[0].astype(F32)

    @pl.when(pl.program_id(1) == 1)
    def _():
        out_ref[...] = other_ref[0].astype(F32)


def spread(own, other, c, axis):
    count, high, wide = own.shape
    shape = {
        0: (high * 2 * count, wide),
        1: (high, wide * 2 * count),
        2: (high * 2, wide * count),
    }[axis]

    def out_place(i, side, place):
        core = (place[0] + side) % 2
        return [(2 * i + core, 0), (0, 2 * i + core), (core, i)][axis]

    return pl.pallas_call(
        spread_kernel,
        grid_spec=pltpu.PrefetchScalarGridSpec(
            num_scalar_prefetch=1,
            grid=(count, 2),
            in_specs=[pl.BlockSpec((1, high, wide), lambda i, side, place: (i, 0, 0))] * 2,
            out_specs=pl.BlockSpec((high, wide), out_place),
        ),
        out_shape=jax.ShapeDtypeStruct(shape, F32),
        compiler_params=pltpu.CompilerParams(vmem_limit_bytes=48 << 20),
        cost_estimate=cost(
            flops=own.size, transcendentals=0, bytes_accessed=12 * own.size
        ),
        name="spread",
    )(c.astype(jnp.int32)[None], own, other)


def dot(left, right):
    return jnp.dot(left, right, preferred_element_type=F32)


def dot_t(left, right):
    return lax.dot_general(left, right, (((1,), (1,)), ((), ())), preferred_element_type=F32)


def t_dot(left, right):
    return lax.dot_general(left, right, (((0,), (0,)), ((), ())), preferred_element_type=F32)


def exchange(field):
    return lax.all_to_all(field, "fsdp", split_axis=0, concat_axis=0, tiled=True)


def by_core(own, other, axis):
    first = lax.axis_index("core") == 0
    return jnp.stack([jnp.where(first, own, other), jnp.where(first, other, own)], axis)


def take(field, index, size, axis):
    return lax.dynamic_slice_in_dim(field, index * size, size, axis)


def body(
    tokens,
    positions,
    gain_attn,
    w_query,
    w_key,
    w_value,
    w_out,
    gain_ffn,
    w_gate,
    w_up,
    w_down,
    grad_out,
):
    seq_count, span, width = tokens.shape
    rows = seq_count * span
    count = lax.axis_size("fsdp")
    depth = lax.axis_size("zed")
    f = lax.axis_index("fsdp")
    z = lax.axis_index("zed")
    c = lax.axis_index("core")
    shard = width // count
    half_shard = shard // 2
    q_width = HEADS * HEAD_DIM // count
    k_width = KV_HEADS * HEAD_DIM // count
    kv_local = KV_HEADS // count
    ff = w_gate.shape[1]
    ff_half = ff // count // 2
    place = jnp.stack([z, c]).astype(jnp.int32)

    x_own = tokens.reshape(rows, width)
    x_list = gather_rel(x_own)
    small = jnp.concatenate(
        [gain_attn.astype(F32), gain_ffn.astype(F32), positions.reshape(rows).astype(F32)]
    ).reshape(-1, LANES)
    small_list = [small] + [xor_send(small, r) for r in range(1, count)]
    gain_rows = shard // LANES

    def by_index(pieces):
        bit = 1
        while bit < count:
            odd = (f // bit) % 2 == 1
            pieces = [jnp.where(odd, pieces[i ^ bit], pieces[i]) for i in range(count)]
            bit *= 2
        return jnp.concatenate(pieces, 0)

    gain_one = by_index([piece[:gain_rows] for piece in small_list]).reshape(1, width)
    gain_two = by_index([piece[gain_rows : 2 * gain_rows] for piece in small_list]).reshape(
        1, width
    )
    places = jnp.concatenate([piece[2 * gain_rows :].reshape(rows) for piece in small_list])
    half_dim = HEAD_DIM // 2
    lane = jnp.arange(LANES, dtype=jnp.int32)
    freqs = jnp.exp((lane % half_dim).astype(F32) * (-2.0 * theta_log / (2 * half_dim)))
    angles = places[:, None] * freqs
    cos_tab = jnp.cos(angles)
    sin_tab = jnp.sin(angles) * jnp.where(lane % HEAD_DIM < half_dim, -1.0, 1.0)

    all_width = q_width + 2 * k_width
    w_own = exchange(pick_heads(place, w_query, w_key, w_value, count))
    w_other = core_swap(w_own)

    w0, x_list, cos_tab, sin_tab, gain_one = lax.optimization_barrier(
        (pick_units(place, w_gate, w_up, count), x_list, cos_tab, sin_tab, gain_one)
    )
    w0 = exchange(w0).reshape(width, ff_half)

    kv_width = 2 * k_width
    h_list, q_list, kv_list = [], [], []
    for r in range(count):
        piece = slice(r * rows, (r + 1) * rows)
        h, q, kv = project(
            place, x_list[r], gain_one, w_own, w_other, cos_tab[piece], sin_tab[piece], kv_width
        )
        h_list.append(h)
        q_list.append(q)
        kv_list.append(kv)
    h_all = jnp.concatenate(h_list, 0)
    q_all = jnp.concatenate(q_list, 0)
    stream = jnp.concatenate(kv_list, 0)
    kv_all = []
    for step in range(depth):
        if step == 0:
            stream, w0 = lax.optimization_barrier((stream, w0))
        if step:
            stream = z_up(stream)
        kv_all += [stream, core_swap(stream)]
    w1, _ = lax.optimization_barrier((w0, stream))
    w1 = lax.ppermute(w1, "zed", [(i, i ^ 1) for i in range(depth)])
    cot_own = grad_out.reshape(rows, width)
    cot_abs, _ = lax.optimization_barrier((cot_own, w0))
    cot_abs = lax.all_gather(cot_abs, "fsdp", axis=0, tiled=True)
    q_all, cot_abs = lax.optimization_barrier((q_all, cot_abs))
    attended, lse = attend(place, q_all, kv_all, span)

    w0 = [w0, core_swap(w0)]

    def chunk(field, r):
        return field[r * rows : (r + 1) * rows]

    branch = [dot(chunk(attended, r), w_out) for r in range(count)]
    branch = reduce_rel([branch[0]] + [part.astype(BF) for part in branch[1:]])
    x_float = x_own.astype(F32)
    resid = x_float + branch
    inv_two = lax.rsqrt(jnp.mean(resid * resid, -1, keepdims=True) + norm_eps)
    resid_hat = resid * inv_two
    h2_list = gather_rel((resid_hat * gain_two).astype(BF))
    h2_list, w1 = lax.optimization_barrier((h2_list, w1))
    h2_all = jnp.concatenate(h2_list, 0)
    w1 = [w1, core_swap(w1)]

    cot_all = jnp.concatenate([take(cot_abs, f ^ r, rows, 0) for r in range(count)], 0)
    hidden, d_gate, d_up = zip(
        *[feed(place, h2_all, cot_all, w0[side], w1[side], w_down, side) for side in range(2)]
    )
    middle = count // 2 * rows
    far = unfeed(place, d_gate, d_up, w0, w1, middle, count * rows)
    near = unfeed(place, d_gate, d_up, w0, w1, 0, middle)
    d_h2 = reduce_rel([chunk(part, r) for part in (near, far) for r in range(count // 2)])
    down = lower(place, hidden, w_down)

    def core_sum(own, other):
        return add_low(own, core_swap(other))

    def halves(left, right):
        cut = left.shape[1] // 2
        return [
            core_sum(*[t_dot(left[:, cols], right[side]).astype(BF) for side in range(2)])
            for cols in (slice(0, cut), slice(cut, 2 * cut))
        ]

    line = Line()
    gate_parts = halves(h2_all, d_gate)
    d_h2, down = line.round((d_h2, down), gate0=gate_parts[0])
    up_parts = halves(h2_all, d_up)
    down_part = core_sum(*[t_dot(hidden[side], cot_all).astype(BF) for side in range(2)])

    d_hat_two = d_h2 * gain_two
    part_gain_two = jnp.sum(d_h2 * resid_hat, 0)
    d_resid = cot_own.astype(F32) + inv_two * (
        d_hat_two - resid_hat * jnp.mean(d_hat_two * resid_hat, -1, keepdims=True)
    )
    d_branch = gather_rel(d_resid.astype(BF))
    d_branch = line.round(d_branch, gate1=gate_parts[1])
    d_branch = jnp.concatenate(d_branch, 0)
    d_attended = dot_t(d_branch, w_out).astype(BF)
    dq, dkv_all = attend_back(place, q_all, d_attended, lse, kv_all, span)
    dq, dkv_all = line.round((dq, dkv_all), up0=up_parts[0])
    d_q = unrotate(dq, cos_tab, sin_tab, rows)
    tail = None
    for step in reversed(range(depth)):
        here = dkv_all[2 * step].astype(F32) + core_swap(dkv_all[2 * step + 1]).astype(F32)
        if tail is not None:
            here = here + z_down(tail).astype(F32)
        tail = here.astype(BF)
    down = reduce_rel([chunk(down, r) for r in range(count)])
    layer_out = (resid + down).astype(BF).reshape(seq_count, span, width)
    tail, up_last, layer_out = line.hold((tail, up_parts[1], layer_out))
    d_kv, d_h1_all = unproject(place, d_q, tail, w_own, w_other, cos_tab, sin_tab)
    d_h1 = reduce_rel([chunk(d_h1_all, r) for r in range(count)])
    d_h1 = line.round(d_h1, up1=up_last)

    def row_halves(field):
        field = field.astype(BF).reshape(count, 2, half_shard, -1)
        own = lax.dynamic_index_in_dim(field, c, 1, keepdims=False)
        other = lax.dynamic_index_in_dim(field, 1 - c, 1, keepdims=False)
        return core_sum(own, other)

    g_q = row_halves(t_dot(h_all, d_q))
    g_kv = t_dot(h_all, d_kv)
    g_out = t_dot(attended, d_branch).astype(BF)
    out_half = q_width // 2
    g_out = core_sum(take(g_out, c, out_half, 0), take(g_out, 1 - c, out_half, 0))

    inv_one = lax.rsqrt(jnp.mean(x_float * x_float, -1, keepdims=True) + norm_eps)
    x_hat = x_float * inv_one
    d_hat_one = d_h1 * gain_one
    part_gain_one = jnp.sum(d_h1 * x_hat, 0)
    d_input = d_resid + inv_one * (
        d_hat_one - x_hat * jnp.mean(d_hat_one * x_hat, -1, keepdims=True)
    )
    grad_tokens = d_input.astype(BF).reshape(seq_count, span, width)
    gains = jnp.stack([part_gain_one, part_gain_two], 1)
    gains = jnp.pad(gains, ((0, 0), (0, LANES - 2)))
    g_kv = row_halves(jnp.concatenate([g_kv, gains], 1))

    def pair_rows(own):
        return spread(own[None], core_swap(own)[None], c, 0)

    def to_rows(own):
        own = exchange(own.reshape(count, shard, ff_half))
        return spread(own, core_swap(own), c, 1)

    cut = ff_half // 2
    d_h1 = line.round(d_h1, down0=down_part[:cut])
    d_h1 = line.round(d_h1, down1=down_part[cut:])

    def whole(name):
        return jnp.concatenate(line.take(name + "0", name + "1"), 0)

    grad_gate = to_rows(whole("gate"))
    grad_gate = line.round(grad_gate, q=g_q, out=g_out, kv=g_kv)
    grad_up = to_rows(whole("up"))
    grad_gate, grad_up = line.round((grad_gate, grad_up))
    grad_gate, grad_up = line.round((grad_gate, grad_up))
    g_q, g_out, g_kv = line.take("q", "out", "kv")
    grad_down = pair_rows(whole("down"))
    grad_out_w = pair_rows(g_out)
    g_q = exchange(g_q)
    grad_q = spread(g_q, core_swap(g_q), c, 2)
    g_kv = exchange(g_kv)
    g_kv = by_core(g_kv, core_swap(g_kv), 0).astype(F32)
    g_kv = jnp.transpose(g_kv, (0, 2, 1, 3)).reshape(shard, count, -1)
    gains = jnp.sum(g_kv[:, :, 2 * k_width : 2 * k_width + 2], 1)
    g_kv = g_kv[:, :, : 2 * k_width].reshape(shard, count * kv_local, 2, HEAD_DIM)
    grad_k = g_kv[:, :, 0].reshape(shard, count * k_width)
    grad_v = g_kv[:, :, 1].reshape(shard, count * k_width)
    return (
        layer_out,
        grad_tokens,
        gains[:, 0],
        grad_q,
        grad_k,
        grad_v,
        grad_out_w,
        gains[:, 1],
        grad_gate,
        grad_up,
        grad_down,
    )


def solution(mesh):
    fsdp, seq = mesh.devices.shape
    split = Mesh(mesh.devices.reshape(fsdp, seq // 2, 2), ("fsdp", "zed", "core"))
    field = P("fsdp", ("zed", "core"), None)
    vector = P("fsdp")
    matrix = P("fsdp", None)
    return jax.shard_map(
        body,
        mesh=split,
        in_specs=(
            field,
            P("fsdp", ("zed", "core")),
            vector,
            matrix,
            matrix,
            matrix,
            matrix,
            vector,
            matrix,
            matrix,
            matrix,
            field,
        ),
        out_specs=(
            field,
            field,
            vector,
            matrix,
            matrix,
            matrix,
            matrix,
            vector,
            matrix,
            matrix,
            matrix,
        ),
        check_vma=False,
    )
```

```python
import functools
import math

import jax
import jax.numpy as jnp
import numpy as np
from jax import lax
from jax.experimental import pallas as pl
from jax.experimental.pallas import tpu as pltpu
from jax.sharding import Mesh
from jax.sharding import PartitionSpec as P

HEADS = 32
KV_HEADS = 8
HEAD_DIM = 64
GROUP = HEADS // KV_HEADS
LANES = 128

norm_eps = 1e-05
theta_log = math.log(500000.0)
BF = jnp.bfloat16
F32 = jnp.float32


def xor_send(field, bit):
    count = lax.axis_size("fsdp")
    return lax.ppermute(field, "fsdp", [(i, i ^ bit) for i in range(count)])


def core_swap(field):
    return lax.ppermute(field, "core", [(0, 1), (1, 0)])


def gather_rel(own, tie=()):
    count = lax.axis_size("fsdp")
    chunks = [own, xor_send(own, 1)]
    if count == 4:
        chunks.append(xor_send(own, 2))
    chunks, tie = lax.optimization_barrier((chunks, tie))
    if count == 4:
        half = own.shape[0] // 2
        top = xor_send(chunks[1][:half], 2)
        low = xor_send(chunks[2][half:], 1)
        return chunks + [jnp.concatenate([top, low], 0)], tie
    bit = 2
    while bit < count:
        chunks = chunks + [xor_send(chunk, bit) for chunk in chunks]
        bit *= 2
    return chunks, tie


def reduce_rel(partials):
    count = lax.axis_size("fsdp")
    if count == 4:
        zero, one, two, three = partials
        half = three.shape[0] // 2
        top = xor_send(three[:half], 1)
        low = xor_send(three[half:], 2)
        two = jnp.concatenate([add_low(two[:half], top), two[half:]], 0)
        one = jnp.concatenate([one[:half], add_low(one[half:], low)], 0)
        one = xor_send(one, 1)
        two = xor_send(two, 2)
        return zero.astype(F32) + one.astype(F32) + two.astype(F32)
    chunks = list(partials)
    bit = count // 2
    while bit >= 1:
        sent = [xor_send(chunks[bit + i].astype(BF), bit) for i in range(bit)]
        chunks = [chunks[i].astype(F32) + sent[i].astype(F32) for i in range(bit)]
        bit //= 2
    return chunks[0]


def add_low(left, right):
    return (left.astype(F32) + right.astype(F32)).astype(BF)


def z_steps():
    count = lax.axis_size("zed")
    half = count // 2
    inwards = [[(i, i + 1), (count - 1 - i, count - 2 - i)] for i in range(half - 1)]
    outwards = [[(b, a) for a, b in pairs] for pairs in reversed(inwards)]
    middle = [(half - 1, half), (half, half - 1)]
    return [(pairs, True) for pairs in inwards + [middle]] + [(pairs, False) for pairs in outwards]


def z_move(field, stage):
    return lax.ppermute(field, "zed", z_steps()[stage][0])


def z_join(field, moved, stage):
    pairs, adds = z_steps()[stage]
    if adds:
        return add_low(field, moved)
    place = lax.axis_index("zed")
    return jnp.where((place == pairs[0][1]) | (place == pairs[1][1]), moved, field)


class Line:
    def __init__(self):
        self.last = len(z_steps())
        self.running = []
        self.ready = {}

    def round(self, tie, **fields):
        self.running += [(name, 0, field) for name, field in fields.items()]
        moved = [z_move(field, stage) for _, stage, field in self.running]
        tie, moved = lax.optimization_barrier((tie, moved))
        left = []
        for (name, stage, field), arrived in zip(self.running, moved):
            field = z_join(field, arrived, stage)
            if stage + 1 == self.last:
                self.ready[name] = field
            else:
                left.append((name, stage + 1, field))
        self.running = left
        return tie

    def take(self, *names):
        while not all(name in self.ready for name in names):
            self.round(())
        return [self.ready[name] for name in names]

    def hold(self, tie):
        held = [field for _, _, field in self.running]
        tie, held = lax.optimization_barrier((tie, held))
        self.running = [(name, stage, h) for (name, stage, _), h in zip(self.running, held)]
        return tie


def z_up(field):
    count = lax.axis_size("zed")
    return lax.ppermute(field, "zed", [(i, i + 1) for i in range(count - 1)])


def z_down(field):
    count = lax.axis_size("zed")
    return lax.ppermute(field, "zed", [(i + 1, i) for i in range(count - 1)])


def cost(flops, transcendentals, bytes_accessed):
    return pl.CostEstimate(
        flops=flops // 32, transcendentals=transcendentals // 32, bytes_accessed=bytes_accessed // 32
    )


def rotated(field, cos_tab, sin_tab):
    lane = lax.broadcasted_iota(jnp.int32, field.shape, 1)
    other = jnp.where(
        lane % HEAD_DIM < HEAD_DIM // 2,
        pltpu.roll(field, LANES - HEAD_DIM // 2, 1),
        pltpu.roll(field, HEAD_DIM // 2, 1),
    )
    return field * cos_tab + other * sin_tab


def kv_tables(cos_tab, sin_tab):
    lane = lax.broadcasted_iota(jnp.int32, cos_tab.shape, 1)
    return (
        jnp.where(lane < HEAD_DIM, cos_tab, 1.0),
        jnp.where(lane < HEAD_DIM, sin_tab, 0.0),
    )


def block_lanes(i, core, shard):
    half = shard // 2
    return pl.ds(pl.multiple_of(i * shard + core * half, half), half)


def project_kernel(
    place_ref, x_ref, gain_ref, own_ref, other_ref, cos_ref, sin_ref, h_ref, q_ref, kv_ref
):
    x = x_ref[...].astype(F32)
    inv = lax.rsqrt(jnp.mean(x * x, -1, keepdims=True) + norm_eps)
    h_ref[...] = (x * inv * gain_ref[...]).astype(BF)
    cos_tab = cos_ref[...]
    sin_tab = sin_ref[...]
    kv_cos, kv_sin = kv_tables(cos_tab, sin_tab)
    core = place_ref[1]
    raw = jnp.zeros((x.shape[0], own_ref.shape[2]), F32)
    for i in range(own_ref.shape[0]):
        for ref, side in ((own_ref, core), (other_ref, 1 - core)):
            cols = block_lanes(i, side, 2 * own_ref.shape[1])
            raw = raw + jnp.dot(h_ref[:, cols], ref[i], preferred_element_type=F32)
    q_width = q_ref.shape[1]
    for start in range(0, q_width, LANES):
        part = rotated(raw[:, start : start + LANES], cos_tab, sin_tab)
        q_ref[:, start : start + LANES] = (part * HEAD_DIM**-0.5).astype(BF)
    for start in range(0, kv_ref.shape[1], LANES):
        part = rotated(raw[:, q_width + start : q_width + start + LANES], kv_cos, kv_sin)
        kv_ref[:, start : start + LANES] = part.astype(BF)


def project(place, x, gain, w_own, w_other, cos_tab, sin_tab, kv_width):
    rows, width = x.shape
    all_width = w_own.shape[2]
    q_width = all_width - kv_width
    return pl.pallas_call(
        project_kernel,
        in_specs=[pl.BlockSpec(memory_space=pltpu.SMEM)]
        + [pl.BlockSpec(memory_space=pltpu.VMEM)] * 6,
        out_shape=(
            jax.ShapeDtypeStruct((rows, width), BF),
            jax.ShapeDtypeStruct((rows, q_width), BF),
            jax.ShapeDtypeStruct((rows, kv_width), BF),
        ),
        compiler_params=pltpu.CompilerParams(vmem_limit_bytes=40 << 20),
        cost_estimate=cost(
            flops=2 * rows * width * all_width,
            transcendentals=rows,
            bytes_accessed=4 * rows * width + 2 * width * all_width,
        ),
        name="project",
    )(place, x, gain, w_own, w_other, cos_tab, sin_tab)


def unrotate_kernel(dq_ref, cos_ref, sin_ref, d_ref):
    for start in range(0, dq_ref.shape[1], LANES):
        part = dq_ref[:, start : start + LANES].astype(F32)
        d_ref[:, start : start + LANES] = rotated(part, cos_ref[...], -sin_ref[...]).astype(BF)


def unrotate(dq, cos_tab, sin_tab, block):
    rows, wide = dq.shape
    tables = pl.BlockSpec((block, LANES), lambda i: (i, 0))
    field = pl.BlockSpec((block, wide), lambda i: (i, 0))
    return pl.pallas_call(
        unrotate_kernel,
        grid=(rows // block,),
        in_specs=[field, tables, tables],
        out_specs=field,
        out_shape=jax.ShapeDtypeStruct(dq.shape, BF),
        cost_estimate=cost(
            flops=6 * rows * wide, transcendentals=0, bytes_accessed=6 * rows * wide
        ),
        name="unrotate",
    )(dq, cos_tab, sin_tab)


def unproject_kernel(
    place_ref, dq_ref, dkv_ref, own_ref, other_ref, cos_ref, sin_ref, d_ref, dh_ref
):
    kv_cos, kv_sin = kv_tables(cos_ref[...], -sin_ref[...])
    q_width = dq_ref.shape[1]
    for start in range(0, dkv_ref.shape[1], LANES):
        part = rotated(dkv_ref[:, start : start + LANES].astype(F32), kv_cos, kv_sin)
        d_ref[:, start : start + LANES] = part.astype(BF)
    core = place_ref[1]
    across = (((1,), (1,)), ((), ()))
    for i in range(own_ref.shape[0]):
        for ref, side in ((own_ref, core), (other_ref, 1 - core)):
            cols = block_lanes(i, side, 2 * own_ref.shape[1])
            total = lax.dot_general(
                dq_ref[...], ref[i, :, :q_width], across, preferred_element_type=F32
            )
            total = total + lax.dot_general(
                d_ref[...], ref[i, :, q_width:], across, preferred_element_type=F32
            )
            dh_ref[:, cols] = total.astype(BF)


def unproject(place, dq, dkv, w_own, w_other, cos_tab, sin_tab):
    rows = dq.shape[0]
    count, half, cols = w_own.shape
    width = 2 * count * half
    block = rows // count

    def row_block(wide):
        return pl.BlockSpec((block, wide), lambda i, place: (i, 0))

    weights = pl.BlockSpec(w_own.shape, lambda i, place: (0, 0, 0))
    return pl.pallas_call(
        unproject_kernel,
        grid_spec=pltpu.PrefetchScalarGridSpec(
            num_scalar_prefetch=1,
            grid=(rows // block,),
            in_specs=[
                row_block(dq.shape[1]),
                row_block(dkv.shape[1]),
                weights,
                weights,
                row_block(LANES),
                row_block(LANES),
            ],
            out_specs=(row_block(dkv.shape[1]), row_block(width)),
        ),
        out_shape=(
            jax.ShapeDtypeStruct(dkv.shape, BF),
            jax.ShapeDtypeStruct((rows, width), BF),
        ),
        compiler_params=pltpu.CompilerParams(vmem_limit_bytes=40 << 20),
        cost_estimate=cost(
            flops=2 * rows * width * cols,
            transcendentals=0,
            bytes_accessed=2 * rows * width + 2 * width * cols + 4 * rows * cols,
        ),
        name="unproject",
    )(place, dq, dkv, w_own, w_other, cos_tab, sin_tab)


def pick_units(place, w_even, w_odd, count):
    high, wide = w_even.shape
    units = wide // count // 2

    def kernel(place_ref, even_ref, odd_ref, out_ref):
        even = place_ref[0] % 2 == 0

        @pl.when(even)
        def _():
            out_ref[0] = even_ref[...]

        @pl.when(jnp.logical_not(even))
        def _():
            out_ref[0] = odd_ref[...]

    def columns(parity):
        def index(i, place):
            here = place[0] % 2 == parity
            return (0, jnp.where(here, 2 * i + place[1], 0))

        return pl.BlockSpec((high, units), index)

    return pl.pallas_call(
        kernel,
        grid_spec=pltpu.PrefetchScalarGridSpec(
            num_scalar_prefetch=1,
            grid=(count,),
            in_specs=[columns(0), columns(1)],
            out_specs=pl.BlockSpec((1, high, units), lambda i, place: (i, 0, 0)),
        ),
        out_shape=jax.ShapeDtypeStruct((count, high, units), BF),
        cost_estimate=cost(
            flops=0, transcendentals=0, bytes_accessed=4 * count * high * units
        ),
        name="pick_units",
    )(place, w_even, w_odd)


def pick_heads(place, w_query, w_key, w_value, count):
    high = w_query.shape[0] // 2
    q_width = w_query.shape[1] // count
    k_width = w_key.shape[1] // count

    def kernel(place_ref, q_ref, k_ref, v_ref, out_ref):
        for i in range(count):
            out_ref[i, :, :q_width] = q_ref[:, i * q_width : (i + 1) * q_width]
            for head in range(k_width // HEAD_DIM):
                cols = slice(i * k_width + head * HEAD_DIM, i * k_width + (head + 1) * HEAD_DIM)
                start = q_width + head * LANES
                out_ref[i, :, start : start + LANES] = jnp.concatenate(
                    [k_ref[:, cols], v_ref[:, cols]], 1
                )

    def half(weight):
        return pl.BlockSpec((high, weight.shape[1]), lambda i, place: (place[1], 0))

    all_width = q_width + 2 * k_width
    return pl.pallas_call(
        kernel,
        grid_spec=pltpu.PrefetchScalarGridSpec(
            num_scalar_prefetch=1,
            grid=(1,),
            in_specs=[half(w_query), half(w_key), half(w_value)],
            out_specs=pl.BlockSpec((count, high, all_width), lambda i, place: (0, 0, 0)),
        ),
        out_shape=jax.ShapeDtypeStruct((count, high, all_width), BF),
        cost_estimate=cost(
            flops=0, transcendentals=0, bytes_accessed=4 * count * high * all_width
        ),
        name="pick_heads",
    )(place, w_query, w_key, w_value)


def feed_kernel(place_ref, h_ref, cot_ref, w0_ref, w1_ref, wd_ref, hidden_ref, dg_ref, du_ref):
    high = h_ref.shape[0] // 2

    def run(wg_ref, wu_ref):
        for start in (0, high):
            rows = slice(start, start + high)
            gate = jnp.dot(h_ref[rows], wg_ref[...], preferred_element_type=F32)
            upper = jnp.dot(h_ref[rows], wu_ref[...], preferred_element_type=F32)
            gate_sig = jax.nn.sigmoid(gate)
            gate_act = gate * gate_sig
            hidden_ref[rows] = (gate_act * upper).astype(BF)
            d_hidden = lax.dot_general(
                cot_ref[rows], wd_ref[...], (((1,), (1,)), ((), ())), preferred_element_type=F32
            )
            d_gate = d_hidden * upper * (gate_sig + gate_act * (1.0 - gate_sig))
            dg_ref[rows] = d_gate.astype(BF)
            du_ref[rows] = (d_hidden * gate_act).astype(BF)

    even = place_ref[0] % 2 == 0

    @pl.when(even)
    def _():
        run(w0_ref, w1_ref)

    @pl.when(jnp.logical_not(even))
    def _():
        run(w1_ref, w0_ref)


def feed(place, h_all, cot_all, w0, w1, w_down, side):
    rows, width = h_all.shape
    units = w0.shape[1]
    block = min(256, units)
    steps = units // block
    full = pl.BlockSpec((rows, width), lambda j, place: (0, 0))
    columns = pl.BlockSpec((width, block), lambda j, place: (0, j))
    out = pl.BlockSpec((rows, block), lambda j, place: (0, j))
    return pl.pallas_call(
        feed_kernel,
        grid_spec=pltpu.PrefetchScalarGridSpec(
            num_scalar_prefetch=1,
            grid=(steps,),
            in_specs=[
                full,
                full,
                columns,
                columns,
                pl.BlockSpec(
                    (block, width), lambda j, place: ((place[1] + side) % 2 * steps + j, 0)
                ),
            ],
            out_specs=[out] * 3,
        ),
        out_shape=[jax.ShapeDtypeStruct((rows, units), BF)] * 3,
        compiler_params=pltpu.CompilerParams(vmem_limit_bytes=56 << 20),
        cost_estimate=cost(
            flops=6 * rows * width * units,
            transcendentals=rows * units,
            bytes_accessed=4 * rows * width + 6 * width * units + 6 * rows * units,
        ),
        name="feed",
    )(place, h_all, cot_all, w0, w1, w_down)


def unfeed(place, dg, du, w0, w1, first, last):
    high = last - first
    units = dg[0].shape[1]
    width = w0[0].shape[0]
    block = min(512, width)
    across = (((1,), (1,)), ((), ()))

    def kernel(place_ref, dg0, dg1, du0, du1, w00, w01, w10, w11, out_ref):
        def run(*pairs):
            total = None
            for d_ref, w_ref in pairs:
                part = lax.dot_general(
                    d_ref[...], w_ref[...], across, preferred_element_type=F32
                )
                total = part if total is None else total + part
            out_ref[...] = total.astype(BF)

        even = place_ref[0] % 2 == 0

        @pl.when(even)
        def _():
            run((dg0, w00), (du0, w10), (dg1, w01), (du1, w11))

        @pl.when(jnp.logical_not(even))
        def _():
            run((du0, w00), (dg0, w10), (du1, w01), (dg1, w11))

    return pl.pallas_call(
        kernel,
        grid_spec=pltpu.PrefetchScalarGridSpec(
            num_scalar_prefetch=1,
            grid=(width // block,),
            in_specs=[pl.BlockSpec((high, units), lambda n, place: (first // high, 0))] * 4
            + [pl.BlockSpec((block, units), lambda n, place: (n, 0))] * 4,
            out_specs=pl.BlockSpec((high, block), lambda n, place: (0, n)),
        ),
        out_shape=jax.ShapeDtypeStruct((high, width), BF),
        compiler_params=pltpu.CompilerParams(vmem_limit_bytes=48 << 20),
        cost_estimate=cost(
            flops=8 * high * units * width,
            transcendentals=0,
            bytes_accessed=8 * width * units + 8 * high * units + 2 * high * width,
        ),
        name="unfeed",
    )(place, *dg, *du, *w0, *w1)


def lower(place, hidden, w_down):
    rows, units = hidden[0].shape
    width = w_down.shape[1]
    block = min(512, width)

    def kernel(place_ref, h0, h1, w0, w1, out_ref):
        total = jnp.dot(h0[...], w0[...], preferred_element_type=F32)
        total = total + jnp.dot(h1[...], w1[...], preferred_element_type=F32)
        out_ref[...] = total.astype(BF)

    return pl.pallas_call(
        kernel,
        grid_spec=pltpu.PrefetchScalarGridSpec(
            num_scalar_prefetch=1,
            grid=(width // block,),
            in_specs=[pl.BlockSpec((rows, units), lambda n, place: (0, 0))] * 2
            + [
                pl.BlockSpec((units, block), lambda n, place: (place[1], n)),
                pl.BlockSpec((units, block), lambda n, place: (1 - place[1], n)),
            ],
            out_specs=pl.BlockSpec((rows, block), lambda n, place: (0, n)),
        ),
        out_shape=jax.ShapeDtypeStruct((rows, width), BF),
        compiler_params=pltpu.CompilerParams(vmem_limit_bytes=48 << 20),
        cost_estimate=cost(
            flops=4 * rows * units * width,
            transcendentals=0,
            bytes_accessed=4 * width * units + 4 * rows * units + 2 * rows * width,
        ),
        name="lower",
    )(place, *hidden, w_down, w_down)


def low_lanes(shape):
    return lax.broadcasted_iota(jnp.int32, shape, 1) < HEAD_DIM


def stack_heads(ref, group, upper):
    rows = []
    for head in range(0, GROUP, 2):
        start = (group * GROUP + head) * HEAD_DIM
        pair = ref[:, start : start + LANES].astype(F32)
        turned = pltpu.roll(pair, HEAD_DIM, 1)
        keep = low_lanes(pair.shape)
        if upper:
            keep = jnp.logical_not(keep)
            rows += [jnp.where(keep, turned, 0.0), jnp.where(keep, pair, 0.0)]
        else:
            rows += [jnp.where(keep, pair, 0.0), jnp.where(keep, turned, 0.0)]
    return jnp.concatenate(rows, 0).astype(BF)


def unstack_heads(stacked, ref, group, upper):
    span = ref.shape[0]
    for head in range(0, GROUP, 2):
        even = stacked[head * span : (head + 1) * span]
        odd = stacked[(head + 1) * span : (head + 2) * span]
        keep = low_lanes(even.shape)
        if upper:
            pair = jnp.where(keep, pltpu.roll(even, HEAD_DIM, 1), odd)
        else:
            pair = jnp.where(keep, even, pltpu.roll(odd, HEAD_DIM, 1))
        start = (group * GROUP + head) * HEAD_DIM
        ref[:, start : start + LANES] = pair.astype(ref.dtype)


def logits_of(place_ref, q_all, kv_own, kv_rest, span):
    own = lax.dot_general(q_all, kv_own, (((1,), (1,)), ((), ())), preferred_element_type=F32)
    rest = lax.dot_general(q_all, kv_rest, (((1,), (1,)), ((), ())), preferred_element_type=F32)
    row = lax.broadcasted_iota(jnp.int32, own.shape, 0) % span
    col = lax.broadcasted_iota(jnp.int32, own.shape, 1)
    own = jnp.where(col <= row, own, -1e30)
    depth = rest.shape[1] // span // 2 + 1
    block = lax.broadcasted_iota(jnp.int32, (1, rest.shape[1]), 1) // span + 1
    have = jnp.where(block == depth, place_ref[1], place_ref[0])
    need = jnp.where(block == depth, 1, block % depth)
    rest = rest + jnp.where(have >= need, 0.0, -1e30)
    return own, rest


def rest_of(kv_refs, cols):
    sibling = kv_refs[-1]
    parts = [ref[:, cols] for ref in kv_refs[1:-1]]
    parts += [sibling[i, :, cols] for i in range(sibling.shape[0])]
    return jnp.concatenate(parts, 0)


def attend_kernel(place_ref, q_ref, *refs):
    kv_refs = refs[:-2]
    out_ref, lse_ref = refs[-2:]
    span = q_ref.shape[0]
    for group in range(lse_ref.shape[1]):
        cols = slice(group * LANES, (group + 1) * LANES)
        q_all = stack_heads(q_ref, group, False)
        kv_own = kv_refs[0][:, cols]
        kv_rest = rest_of(kv_refs, cols)
        own, rest = logits_of(place_ref, q_all, kv_own, kv_rest, span)
        top = jnp.maximum(jnp.max(own, -1, keepdims=True), jnp.max(rest, -1, keepdims=True))
        own = jnp.exp(own - top)
        rest = jnp.exp(rest - top)
        total = jnp.sum(own, -1, keepdims=True) + jnp.sum(rest, -1, keepdims=True)
        out = jnp.dot(own.astype(BF), kv_own, preferred_element_type=F32)
        out = out + jnp.dot(rest.astype(BF), kv_rest, preferred_element_type=F32)
        unstack_heads(out / total, out_ref, group, True)
        lse_ref[0, group] = top + jnp.log(total)


def attend_back_kernel(place_ref, q_ref, do_ref, lse_ref, *refs):
    count = (len(refs) - 1) // 2
    kv_refs = refs[:count]
    dq_ref = refs[count]
    dkv_refs = refs[count + 1 :]
    span = q_ref.shape[0]
    flip = (((0,), (0,)), ((), ()))
    across = (((1,), (1,)), ((), ()))
    for group in range(lse_ref.shape[1]):
        cols = slice(group * LANES, (group + 1) * LANES)
        q_all = stack_heads(q_ref, group, False)
        do_all = stack_heads(do_ref, group, True)
        kv_own = kv_refs[0][:, cols]
        kv_rest = rest_of(kv_refs, cols)
        own, rest = logits_of(place_ref, q_all, kv_own, kv_rest, span)
        lse = lse_ref[0, group]
        own = jnp.exp(own - lse)
        rest = jnp.exp(rest - lse)
        d_own = lax.dot_general(do_all, kv_own, across, preferred_element_type=F32)
        d_rest = lax.dot_general(do_all, kv_rest, across, preferred_element_type=F32)
        inner = jnp.sum(own * d_own, -1, keepdims=True) + jnp.sum(rest * d_rest, -1, keepdims=True)
        d_own = (own * (d_own - inner)).astype(BF)
        d_rest = (rest * (d_rest - inner)).astype(BF)
        dq = jnp.dot(d_own, kv_own, preferred_element_type=F32)
        dq = dq + jnp.dot(d_rest, kv_rest, preferred_element_type=F32)
        unstack_heads(dq * HEAD_DIM**-0.5, dq_ref, group, False)
        dkv = lax.dot_general(d_own, q_all, flip, preferred_element_type=F32)
        dkv = dkv + lax.dot_general(own.astype(BF), do_all, flip, preferred_element_type=F32)
        dkv_refs[0][:, cols] = dkv.astype(BF)
        dkv = lax.dot_general(d_rest, q_all, flip, preferred_element_type=F32)
        dkv = dkv + lax.dot_general(rest.astype(BF), do_all, flip, preferred_element_type=F32)
        for i in range(count - 2):
            dkv_refs[i + 1][:, cols] = dkv[i * span : (i + 1) * span].astype(BF)
        for i in range(count - 1):
            start = (count - 2 + i) * span
            dkv_refs[-1][i, :, cols] = dkv[start : start + span].astype(BF)


def attend_specs(q_all, kv_all, span):
    depth, _, kv_width = kv_all[-1].shape
    groups = kv_width // LANES
    kv_spec = pl.BlockSpec((span, kv_width), lambda i, place: (i, 0))
    sibling = pl.BlockSpec((depth, span, kv_width), lambda i, place: (0, i, 0))
    return (
        pl.BlockSpec((span, q_all.shape[1]), lambda i, place: (i, 0)),
        [kv_spec] * depth + [sibling],
        pl.BlockSpec((1, groups, GROUP * span, 1), lambda i, place: (i, 0, 0, 0)),
        groups,
    )


def attend(place, q_all, kv_all, span):
    rows = q_all.shape[0]
    q_spec, kv_specs, lse_spec, groups = attend_specs(q_all, kv_all, span)
    cells = rows * groups * GROUP * span * (2 * len(kv_all) - 2)
    return pl.pallas_call(
        attend_kernel,
        grid_spec=pltpu.PrefetchScalarGridSpec(
            num_scalar_prefetch=1,
            grid=(rows // span,),
            in_specs=[q_spec] + kv_specs,
            out_specs=[q_spec, lse_spec],
        ),
        out_shape=(
            jax.ShapeDtypeStruct(q_all.shape, BF),
            jax.ShapeDtypeStruct((rows // span, groups, GROUP * span, 1), F32),
        ),
        compiler_params=pltpu.CompilerParams(vmem_limit_bytes=56 << 20),
        cost_estimate=cost(
            flops=2 * 4 * LANES * cells, transcendentals=cells, bytes_accessed=16 << 20
        ),
        name="attend",
    )(place, q_all, *kv_all)


def attend_back(place, q_all, do_all, lse, kv_all, span):
    rows = q_all.shape[0]
    q_spec, kv_specs, lse_spec, groups = attend_specs(q_all, kv_all, span)
    cells = rows * groups * GROUP * span * (2 * len(kv_all) - 2)
    outs = pl.pallas_call(
        attend_back_kernel,
        grid_spec=pltpu.PrefetchScalarGridSpec(
            num_scalar_prefetch=1,
            grid=(rows // span,),
            in_specs=[q_spec, q_spec, lse_spec] + kv_specs,
            out_specs=[q_spec] + kv_specs,
        ),
        out_shape=[jax.ShapeDtypeStruct(q_all.shape, BF)]
        + [jax.ShapeDtypeStruct(kv.shape, BF) for kv in kv_all],
        compiler_params=pltpu.CompilerParams(vmem_limit_bytes=60 << 20),
        cost_estimate=cost(
            flops=2 * 8 * LANES * cells, transcendentals=cells, bytes_accessed=24 << 20
        ),
        name="attend_back",
    )(place, q_all, do_all, lse, *kv_all)
    return outs[0], outs[1:]


def spread_kernel(place_ref, own_ref, other_ref, out_ref):
    @pl.when(pl.program_id(1) == 0)
    def _():
        out_ref[...] = own_ref[0].astype(F32)

    @pl.when(pl.program_id(1) == 1)
    def _():
        out_ref[...] = other_ref[0].astype(F32)


def spread(own, other, c, axis):
    count, high, wide = own.shape
    shape = {
        0: (high * 2 * count, wide),
        1: (high, wide * 2 * count),
        2: (high * 2, wide * count),
    }[axis]

    def out_place(i, side, place):
        core = (place[0] + side) % 2
        return [(2 * i + core, 0), (0, 2 * i + core), (core, i)][axis]

    return pl.pallas_call(
        spread_kernel,
        grid_spec=pltpu.PrefetchScalarGridSpec(
            num_scalar_prefetch=1,
            grid=(count, 2),
            in_specs=[pl.BlockSpec((1, high, wide), lambda i, side, place: (i, 0, 0))] * 2,
            out_specs=pl.BlockSpec((high, wide), out_place),
        ),
        out_shape=jax.ShapeDtypeStruct(shape, F32),
        compiler_params=pltpu.CompilerParams(vmem_limit_bytes=48 << 20),
        cost_estimate=cost(
            flops=own.size, transcendentals=0, bytes_accessed=12 * own.size
        ),
        name="spread",
    )(c.astype(jnp.int32)[None], own, other)


def dot(left, right):
    return jnp.dot(left, right, preferred_element_type=F32)


def dot_t(left, right):
    return lax.dot_general(left, right, (((1,), (1,)), ((), ())), preferred_element_type=F32)


def t_dot(left, right):
    return lax.dot_general(left, right, (((0,), (0,)), ((), ())), preferred_element_type=F32)


def exchange(field):
    return lax.all_to_all(field, "fsdp", split_axis=0, concat_axis=0, tiled=True)


def by_core(own, other, axis):
    first = lax.axis_index("core") == 0
    return jnp.stack([jnp.where(first, own, other), jnp.where(first, other, own)], axis)


def take(field, index, size, axis):
    return lax.dynamic_slice_in_dim(field, index * size, size, axis)


def body(
    tokens,
    positions,
    gain_attn,
    w_query,
    w_key,
    w_value,
    w_out,
    gain_ffn,
    w_gate,
    w_up,
    w_down,
    grad_out,
):
    seq_count, span, width = tokens.shape
    rows = seq_count * span
    count = lax.axis_size("fsdp")
    depth = lax.axis_size("zed")
    f = lax.axis_index("fsdp")
    z = lax.axis_index("zed")
    c = lax.axis_index("core")
    shard = width // count
    half_shard = shard // 2
    q_width = HEADS * HEAD_DIM // count
    k_width = KV_HEADS * HEAD_DIM // count
    kv_local = KV_HEADS // count
    ff = w_gate.shape[1]
    ff_half = ff // count // 2
    place = jnp.stack([z, c]).astype(jnp.int32)

    x_own = tokens.reshape(rows, width)
    x_list, _ = gather_rel(x_own)
    small = jnp.concatenate(
        [gain_attn.astype(F32), gain_ffn.astype(F32), positions.reshape(rows).astype(F32)]
    ).reshape(-1, LANES)
    small_list = [small] + [xor_send(small, r) for r in range(1, count)]
    gain_rows = shard // LANES

    def by_index(pieces):
        bit = 1
        while bit < count:
            odd = (f // bit) % 2 == 1
            pieces = [jnp.where(odd, pieces[i ^ bit], pieces[i]) for i in range(count)]
            bit *= 2
        return jnp.concatenate(pieces, 0)

    gain_one = by_index([piece[:gain_rows] for piece in small_list]).reshape(1, width)
    gain_two = by_index([piece[gain_rows : 2 * gain_rows] for piece in small_list]).reshape(
        1, width
    )
    places = jnp.concatenate([piece[2 * gain_rows :].reshape(rows) for piece in small_list])
    half_dim = HEAD_DIM // 2
    lane = jnp.arange(LANES, dtype=jnp.int32)
    freqs = jnp.exp((lane % half_dim).astype(F32) * (-2.0 * theta_log / (2 * half_dim)))
    angles = places[:, None] * freqs
    cos_tab = jnp.cos(angles)
    sin_tab = jnp.sin(angles) * jnp.where(lane % HEAD_DIM < half_dim, -1.0, 1.0)

    all_width = q_width + 2 * k_width
    w_own = exchange(pick_heads(place, w_query, w_key, w_value, count))
    w_other = core_swap(w_own)

    w0, x_list, cos_tab, sin_tab, gain_one = lax.optimization_barrier(
        (pick_units(place, w_gate, w_up, count), x_list, cos_tab, sin_tab, gain_one)
    )
    w0 = exchange(w0).reshape(width, ff_half)

    kv_width = 2 * k_width
    h_list, q_list, kv_list = [], [], []
    for r in range(count):
        piece = slice(r * rows, (r + 1) * rows)
        h, q, kv = project(
            place, x_list[r], gain_one, w_own, w_other, cos_tab[piece], sin_tab[piece], kv_width
        )
        h_list.append(h)
        q_list.append(q)
        kv_list.append(kv)
    h_all = jnp.concatenate(h_list, 0)
    q_all = jnp.concatenate(q_list, 0)
    stream = jnp.concatenate(kv_list, 0)
    kv_all = [stream]
    sibling = core_swap(stream)
    for step in range(1, depth):
        stream = z_up(stream)
        if step == 1:
            stream, w0 = lax.optimization_barrier((stream, w0))
        kv_all.append(stream)
    others = core_swap(jnp.stack(kv_all[1:]))
    kv_all = kv_all + [jnp.concatenate([sibling[None], others], 0)]
    w1, _ = lax.optimization_barrier((w0, stream))
    w1 = lax.ppermute(w1, "zed", [(i, i ^ 1) for i in range(depth)])
    cot_own = grad_out.reshape(rows, width)
    cot_abs, _ = lax.optimization_barrier((cot_own, w0))
    cot_abs = lax.all_gather(cot_abs, "fsdp", axis=0, tiled=True)
    attended, lse = attend(place, q_all, kv_all, span)
    w0 = [w0, core_swap(w0)]
    attended, cot_abs, w0 = lax.optimization_barrier((attended, cot_abs, w0))


    def chunk(field, r):
        return field[r * rows : (r + 1) * rows]

    branch = [dot(chunk(attended, r), w_out) for r in range(count)]
    branch = reduce_rel([branch[0]] + [part.astype(BF) for part in branch[1:]])
    x_float = x_own.astype(F32)
    resid = x_float + branch
    inv_two = lax.rsqrt(jnp.mean(resid * resid, -1, keepdims=True) + norm_eps)
    resid_hat = resid * inv_two
    h2_list, w1 = gather_rel((resid_hat * gain_two).astype(BF), w1)
    h2_all = jnp.concatenate(h2_list, 0)
    w1 = [w1, core_swap(w1)]

    cot_all = jnp.concatenate([take(cot_abs, f ^ r, rows, 0) for r in range(count)], 0)
    hidden, d_gate, d_up = zip(
        *[feed(place, h2_all, cot_all, w0[side], w1[side], w_down, side) for side in range(2)]
    )
    middle = count // 2 * rows
    far = unfeed(place, d_gate, d_up, w0, w1, middle, count * rows)
    near = unfeed(place, d_gate, d_up, w0, w1, 0, middle)
    def core_sum(own, other):
        return add_low(own, core_swap(other))

    def halves(left, right):
        cut = left.shape[1] // 2
        other = core_swap(t_dot(left, right[1]).astype(BF))
        return [
            (t_dot(left[:, rows], right[0]) + other[rows].astype(F32)).astype(BF)
            for rows in (slice(0, cut), slice(cut, 2 * cut))
        ]

    near, late = lax.optimization_barrier((near, (h2_all, hidden, cot_all, d_up)))
    d_h2 = reduce_rel([chunk(part, r) for part in (near, far) for r in range(count // 2)])
    down = lower(place, hidden, w_down)
    line = Line()
    gate_parts = halves(h2_all, d_gate)
    d_h2, down = line.round((d_h2, down), gate0=gate_parts[0])
    h2_late, hidden_late, cot_late, d_up_late = late
    up_parts = halves(h2_late, d_up_late)
    down_part = core_sum(*[t_dot(hidden_late[side], cot_late).astype(BF) for side in range(2)])

    d_hat_two = d_h2 * gain_two
    part_gain_two = jnp.sum(d_h2 * resid_hat, 0)
    d_resid = cot_own.astype(F32) + inv_two * (
        d_hat_two - resid_hat * jnp.mean(d_hat_two * resid_hat, -1, keepdims=True)
    )
    d_branch, _ = gather_rel(d_resid.astype(BF))
    d_branch = line.round(d_branch, gate1=gate_parts[1])
    d_branch = jnp.concatenate(d_branch, 0)
    d_attended = dot_t(d_branch, w_out).astype(BF)
    dq, dkv_all = attend_back(place, q_all, d_attended, lse, kv_all, span)
    dq, dkv_all, down = line.round((dq, dkv_all, down), up0=up_parts[0])
    d_q = unrotate(dq, cos_tab, sin_tab, rows)
    up_last = up_parts[1]
    tail = None
    from_sibling = core_swap(dkv_all[-1])
    for step in reversed(range(depth)):
        here = dkv_all[step].astype(F32) + from_sibling[step].astype(F32)
        if tail is not None:
            moved = z_down(tail)
            if step == depth - 2:
                moved, up_last = line.hold((moved, up_last))
            here = here + moved.astype(F32)
        tail = here.astype(BF)
    down = reduce_rel([chunk(down, r) for r in range(count)])
    layer_out = (resid + down).astype(BF).reshape(seq_count, span, width)
    tail, layer_out = line.round((tail, layer_out), up1=up_last)
    def row_pair(field):
        field = field.astype(BF).reshape(count, 2, half_shard, -1)
        own = lax.dynamic_index_in_dim(field, c, 1, keepdims=False)
        other = lax.dynamic_index_in_dim(field, 1 - c, 1, keepdims=False)
        return own, other

    g_q = row_pair(t_dot(h_all, d_q))
    g_out = t_dot(attended, d_branch).astype(BF)
    out_half = q_width // 2
    g_out = (take(g_out, c, out_half, 0), take(g_out, 1 - c, out_half, 0))
    g_qo = core_sum(
        *[
            jnp.concatenate([q.reshape(-1, q_width), out.reshape(-1, q_width)], 0)
            for q, out in zip(g_q, g_out)
        ]
    )
    d_kv, d_h1_all = unproject(place, d_q, tail, w_own, w_other, cos_tab, sin_tab)
    d_h1 = reduce_rel([chunk(d_h1_all, r) for r in range(count)])
    g_kv = core_sum(*row_pair(t_dot(h_all, d_kv)))
    d_h1, g_kv = line.round((d_h1, g_kv), qo=g_qo)

    inv_one = lax.rsqrt(jnp.mean(x_float * x_float, -1, keepdims=True) + norm_eps)
    x_hat = x_float * inv_one
    d_hat_one = d_h1 * gain_one
    part_gain_one = jnp.sum(d_h1 * x_hat, 0)
    d_input = d_resid + inv_one * (
        d_hat_one - x_hat * jnp.mean(d_hat_one * x_hat, -1, keepdims=True)
    )
    grad_tokens = d_input.astype(BF).reshape(seq_count, span, width)
    gains = jnp.stack([part_gain_one, part_gain_two], 1)
    gains = jnp.pad(gains, ((0, 0), (0, LANES - 2)))
    gains = core_sum(*row_pair(gains))

    def pair_rows(own):
        return spread(own[None], core_swap(own)[None], c, 0)

    def to_rows(own):
        own = exchange(own.reshape(count, shard, ff_half))
        return spread(own, core_swap(own), c, 1)

    cut = ff_half // 2
    gains = line.round(gains, kv=g_kv, down0=down_part[:cut])

    def whole(name):
        return jnp.concatenate(line.take(name + "0", name + "1"), 0)

    grad_gate = to_rows(whole("gate"))
    grad_gate = line.round(grad_gate, gains=gains, down1=down_part[cut:])
    grad_up = to_rows(whole("up"))
    (g_qo,) = line.take("qo")
    high = count * half_shard
    grad_out_w = pair_rows(g_qo[high:].reshape(out_half, width))
    g_q = exchange(g_qo[:high].reshape(count, half_shard, q_width))
    grad_q = spread(g_q, core_swap(g_q), c, 2)
    grad_up, grad_out_w, grad_q = line.round((grad_up, grad_out_w, grad_q))
    (g_kv,) = line.take("kv")
    g_kv = exchange(g_kv)
    g_kv = by_core(g_kv, core_swap(g_kv), 0).astype(F32)
    g_kv = jnp.transpose(g_kv, (0, 2, 1, 3)).reshape(shard, count * kv_local, 2, HEAD_DIM)
    grad_k = g_kv[:, :, 0].reshape(shard, count * k_width)
    grad_v = g_kv[:, :, 1].reshape(shard, count * k_width)
    grad_k, grad_v = line.round((grad_k, grad_v))
    (gains,) = line.take("gains")
    gains = exchange(gains)[:, :, :2].astype(F32)
    gains = jnp.sum(gains, 0)
    gains = by_core(gains, core_swap(gains), 0).reshape(shard, 2)
    grad_down = pair_rows(whole("down"))
    return (
        layer_out,
        grad_tokens,
        gains[:, 0],
        grad_q,
        grad_k,
        grad_v,
        grad_out_w,
        gains[:, 1],
        grad_gate,
        grad_up,
        grad_down,
    )


def solution(mesh):
    fsdp, seq = mesh.devices.shape
    split = Mesh(mesh.devices.reshape(fsdp, seq // 2, 2), ("fsdp", "zed", "core"))
    field = P("fsdp", ("zed", "core"), None)
    vector = P("fsdp")
    matrix = P("fsdp", None)
    return jax.shard_map(
        body,
        mesh=split,
        in_specs=(
            field,
            P("fsdp", ("zed", "core")),
            vector,
            matrix,
            matrix,
            matrix,
            matrix,
            vector,
            matrix,
            matrix,
            matrix,
            field,
        ),
        out_specs=(
            field,
            field,
            vector,
            matrix,
            matrix,
            matrix,
            matrix,
            vector,
            matrix,
            matrix,
            matrix,
        ),
        check_vma=False,
    )
```

```python
import functools
import math

import jax
import jax.numpy as jnp
import numpy as np
from jax import lax
from jax.experimental import pallas as pl
from jax.experimental.pallas import tpu as pltpu
from jax.sharding import Mesh
from jax.sharding import PartitionSpec as P

HEADS = 32
KV_HEADS = 8
HEAD_DIM = 64
GROUP = HEADS // KV_HEADS
LANES = 128

norm_eps = 1e-05
theta_log = math.log(500000.0)
BF = jnp.bfloat16
F32 = jnp.float32


def xor_send(field, bit):
    count = lax.axis_size("fsdp")
    return lax.ppermute(field, "fsdp", [(i, i ^ bit) for i in range(count)])


def core_swap(field):
    return lax.ppermute(field, "core", [(0, 1), (1, 0)])


def gather_rel(own, tie=()):
    count = lax.axis_size("fsdp")
    chunks = [own, xor_send(own, 1)]
    if count == 4:
        chunks.append(xor_send(own, 2))
    chunks, tie = lax.optimization_barrier((chunks, tie))
    if count == 4:
        half = own.shape[0] // 2
        top = xor_send(chunks[1][:half], 2)
        low = xor_send(chunks[2][half:], 1)
        return chunks + [jnp.concatenate([top, low], 0)], tie
    bit = 2
    while bit < count:
        chunks = chunks + [xor_send(chunk, bit) for chunk in chunks]
        bit *= 2
    return chunks, tie


def reduce_rel(partials):
    count = lax.axis_size("fsdp")
    if count == 4:
        zero, one, two, three = partials
        half = three.shape[0] // 2
        top = xor_send(three[:half], 1)
        low = xor_send(three[half:], 2)
        two = jnp.concatenate([add_low(two[:half], top), two[half:]], 0)
        one = jnp.concatenate([one[:half], add_low(one[half:], low)], 0)
        one = xor_send(one, 1)
        two = xor_send(two, 2)
        return zero.astype(F32) + one.astype(F32) + two.astype(F32)
    chunks = list(partials)
    bit = count // 2
    while bit >= 1:
        sent = [xor_send(chunks[bit + i].astype(BF), bit) for i in range(bit)]
        chunks = [chunks[i].astype(F32) + sent[i].astype(F32) for i in range(bit)]
        bit //= 2
    return chunks[0]


def add_low(left, right):
    return (left.astype(F32) + right.astype(F32)).astype(BF)


def z_steps():
    count = lax.axis_size("zed")
    half = count // 2
    inwards = [[(i, i + 1), (count - 1 - i, count - 2 - i)] for i in range(half - 1)]
    outwards = [[(b, a) for a, b in pairs] for pairs in reversed(inwards)]
    middle = [(half - 1, half), (half, half - 1)]
    return [(pairs, True) for pairs in inwards + [middle]] + [(pairs, False) for pairs in outwards]


def z_move(field, stage):
    return lax.ppermute(field, "zed", z_steps()[stage][0])


def z_join(field, moved, stage):
    pairs, adds = z_steps()[stage]
    if adds:
        return add_low(field, moved)
    place = lax.axis_index("zed")
    return jnp.where((place == pairs[0][1]) | (place == pairs[1][1]), moved, field)


class Line:
    def __init__(self):
        self.last = len(z_steps())
        self.running = []
        self.ready = {}

    def round(self, tie, **fields):
        self.running += [(name, 0, field) for name, field in fields.items()]
        moved = [z_move(field, stage) for _, stage, field in self.running]
        tie, moved = lax.optimization_barrier((tie, moved))
        left = []
        for (name, stage, field), arrived in zip(self.running, moved):
            field = z_join(field, arrived, stage)
            if stage + 1 == self.last:
                self.ready[name] = field
            else:
                left.append((name, stage + 1, field))
        self.running = left
        return tie

    def take(self, *names):
        while not all(name in self.ready for name in names):
            self.round(())
        return [self.ready[name] for name in names]

    def hold(self, tie):
        held = [field for _, _, field in self.running]
        tie, held = lax.optimization_barrier((tie, held))
        self.running = [(name, stage, h) for (name, stage, _), h in zip(self.running, held)]
        return tie


def z_up(field):
    count = lax.axis_size("zed")
    return lax.ppermute(field, "zed", [(i, i + 1) for i in range(count - 1)])


def z_down(field):
    count = lax.axis_size("zed")
    return lax.ppermute(field, "zed", [(i + 1, i) for i in range(count - 1)])


def cost(flops, transcendentals, bytes_accessed):
    return pl.CostEstimate(
        flops=flops // 32, transcendentals=transcendentals // 32, bytes_accessed=bytes_accessed // 32
    )


def rotated(field, cos_tab, sin_tab):
    lane = lax.broadcasted_iota(jnp.int32, field.shape, 1)
    other = jnp.where(
        lane % HEAD_DIM < HEAD_DIM // 2,
        pltpu.roll(field, LANES - HEAD_DIM // 2, 1),
        pltpu.roll(field, HEAD_DIM // 2, 1),
    )
    return field * cos_tab + other * sin_tab


def kv_tables(cos_tab, sin_tab):
    lane = lax.broadcasted_iota(jnp.int32, cos_tab.shape, 1)
    return (
        jnp.where(lane < HEAD_DIM, cos_tab, 1.0),
        jnp.where(lane < HEAD_DIM, sin_tab, 0.0),
    )


def block_lanes(i, core, shard):
    half = shard // 2
    return pl.ds(pl.multiple_of(i * shard + core * half, half), half)


def project_kernel(
    place_ref, x_ref, gain_ref, own_ref, other_ref, cos_ref, sin_ref, h_ref, q_ref, kv_ref
):
    x = x_ref[...].astype(F32)
    inv = lax.rsqrt(jnp.mean(x * x, -1, keepdims=True) + norm_eps)
    h_ref[...] = (x * inv * gain_ref[...]).astype(BF)
    cos_tab = cos_ref[...]
    sin_tab = sin_ref[...]
    kv_cos, kv_sin = kv_tables(cos_tab, sin_tab)
    core = place_ref[1]
    raw = jnp.zeros((x.shape[0], own_ref.shape[2]), F32)
    for i in range(own_ref.shape[0]):
        for ref, side in ((own_ref, core), (other_ref, 1 - core)):
            cols = block_lanes(i, side, 2 * own_ref.shape[1])
            raw = raw + jnp.dot(h_ref[:, cols], ref[i], preferred_element_type=F32)
    q_width = q_ref.shape[1]
    for start in range(0, q_width, LANES):
        part = rotated(raw[:, start : start + LANES], cos_tab, sin_tab)
        q_ref[:, start : start + LANES] = (part * HEAD_DIM**-0.5).astype(BF)
    for start in range(0, kv_ref.shape[1], LANES):
        part = rotated(raw[:, q_width + start : q_width + start + LANES], kv_cos, kv_sin)
        kv_ref[:, start : start + LANES] = part.astype(BF)


def project(place, x, gain, w_own, w_other, cos_tab, sin_tab, kv_width):
    rows, width = x.shape
    all_width = w_own.shape[2]
    q_width = all_width - kv_width
    return pl.pallas_call(
        project_kernel,
        in_specs=[pl.BlockSpec(memory_space=pltpu.SMEM)]
        + [pl.BlockSpec(memory_space=pltpu.VMEM)] * 6,
        out_shape=(
            jax.ShapeDtypeStruct((rows, width), BF),
            jax.ShapeDtypeStruct((rows, q_width), BF),
            jax.ShapeDtypeStruct((rows, kv_width), BF),
        ),
        compiler_params=pltpu.CompilerParams(vmem_limit_bytes=40 << 20),
        cost_estimate=cost(
            flops=2 * rows * width * all_width,
            transcendentals=rows,
            bytes_accessed=4 * rows * width + 2 * width * all_width,
        ),
        name="project",
    )(place, x, gain, w_own, w_other, cos_tab, sin_tab)


def unrotate_kernel(dq_ref, cos_ref, sin_ref, d_ref):
    for start in range(0, dq_ref.shape[1], LANES):
        part = dq_ref[:, start : start + LANES].astype(F32)
        d_ref[:, start : start + LANES] = rotated(part, cos_ref[...], -sin_ref[...]).astype(BF)


def unrotate(dq, cos_tab, sin_tab, block):
    rows, wide = dq.shape
    tables = pl.BlockSpec((block, LANES), lambda i: (i, 0))
    field = pl.BlockSpec((block, wide), lambda i: (i, 0))
    return pl.pallas_call(
        unrotate_kernel,
        grid=(rows // block,),
        in_specs=[field, tables, tables],
        out_specs=field,
        out_shape=jax.ShapeDtypeStruct(dq.shape, BF),
        cost_estimate=cost(
            flops=6 * rows * wide, transcendentals=0, bytes_accessed=6 * rows * wide
        ),
        name="unrotate",
    )(dq, cos_tab, sin_tab)


def unproject_kernel(
    place_ref, dq_ref, dkv_ref, own_ref, other_ref, cos_ref, sin_ref, d_ref, dh_ref
):
    kv_cos, kv_sin = kv_tables(cos_ref[...], -sin_ref[...])
    q_width = dq_ref.shape[1]
    for start in range(0, dkv_ref.shape[1], LANES):
        part = rotated(dkv_ref[:, start : start + LANES].astype(F32), kv_cos, kv_sin)
        d_ref[:, start : start + LANES] = part.astype(BF)
    core = place_ref[1]
    across = (((1,), (1,)), ((), ()))
    for i in range(own_ref.shape[0]):
        for ref, side in ((own_ref, core), (other_ref, 1 - core)):
            cols = block_lanes(i, side, 2 * own_ref.shape[1])
            total = lax.dot_general(
                dq_ref[...], ref[i, :, :q_width], across, preferred_element_type=F32
            )
            total = total + lax.dot_general(
                d_ref[...], ref[i, :, q_width:], across, preferred_element_type=F32
            )
            dh_ref[:, cols] = total.astype(BF)


def unproject(place, dq, dkv, w_own, w_other, cos_tab, sin_tab):
    rows = dq.shape[0]
    count, half, cols = w_own.shape
    width = 2 * count * half
    block = rows // count

    def row_block(wide):
        return pl.BlockSpec((block, wide), lambda i, place: (i, 0))

    weights = pl.BlockSpec(w_own.shape, lambda i, place: (0, 0, 0))
    return pl.pallas_call(
        unproject_kernel,
        grid_spec=pltpu.PrefetchScalarGridSpec(
            num_scalar_prefetch=1,
            grid=(rows // block,),
            in_specs=[
                row_block(dq.shape[1]),
                row_block(dkv.shape[1]),
                weights,
                weights,
                row_block(LANES),
                row_block(LANES),
            ],
            out_specs=(row_block(dkv.shape[1]), row_block(width)),
        ),
        out_shape=(
            jax.ShapeDtypeStruct(dkv.shape, BF),
            jax.ShapeDtypeStruct((rows, width), BF),
        ),
        compiler_params=pltpu.CompilerParams(vmem_limit_bytes=40 << 20),
        cost_estimate=cost(
            flops=2 * rows * width * cols,
            transcendentals=0,
            bytes_accessed=2 * rows * width + 2 * width * cols + 4 * rows * cols,
        ),
        name="unproject",
    )(place, dq, dkv, w_own, w_other, cos_tab, sin_tab)


def pick_units(place, w_even, w_odd, count):
    high, wide = w_even.shape
    units = wide // count // 2

    def kernel(place_ref, even_ref, odd_ref, out_ref):
        even = place_ref[0] % 2 == 0

        @pl.when(even)
        def _():
            out_ref[0] = even_ref[...]

        @pl.when(jnp.logical_not(even))
        def _():
            out_ref[0] = odd_ref[...]

    def columns(parity):
        def index(i, place):
            here = place[0] % 2 == parity
            return (0, jnp.where(here, 2 * i + place[1], 0))

        return pl.BlockSpec((high, units), index)

    return pl.pallas_call(
        kernel,
        grid_spec=pltpu.PrefetchScalarGridSpec(
            num_scalar_prefetch=1,
            grid=(count,),
            in_specs=[columns(0), columns(1)],
            out_specs=pl.BlockSpec((1, high, units), lambda i, place: (i, 0, 0)),
        ),
        out_shape=jax.ShapeDtypeStruct((count, high, units), BF),
        cost_estimate=cost(
            flops=0, transcendentals=0, bytes_accessed=4 * count * high * units
        ),
        name="pick_units",
    )(place, w_even, w_odd)


def pick_heads(place, w_query, w_key, w_value, count):
    high = w_query.shape[0] // 2
    q_width = w_query.shape[1] // count
    k_width = w_key.shape[1] // count

    def kernel(place_ref, q_ref, k_ref, v_ref, out_ref):
        for i in range(count):
            out_ref[i, :, :q_width] = q_ref[:, i * q_width : (i + 1) * q_width]
            for head in range(k_width // HEAD_DIM):
                cols = slice(i * k_width + head * HEAD_DIM, i * k_width + (head + 1) * HEAD_DIM)
                start = q_width + head * LANES
                out_ref[i, :, start : start + LANES] = jnp.concatenate(
                    [k_ref[:, cols], v_ref[:, cols]], 1
                )

    def half(weight):
        return pl.BlockSpec((high, weight.shape[1]), lambda i, place: (place[1], 0))

    all_width = q_width + 2 * k_width
    return pl.pallas_call(
        kernel,
        grid_spec=pltpu.PrefetchScalarGridSpec(
            num_scalar_prefetch=1,
            grid=(1,),
            in_specs=[half(w_query), half(w_key), half(w_value)],
            out_specs=pl.BlockSpec((count, high, all_width), lambda i, place: (0, 0, 0)),
        ),
        out_shape=jax.ShapeDtypeStruct((count, high, all_width), BF),
        cost_estimate=cost(
            flops=0, transcendentals=0, bytes_accessed=4 * count * high * all_width
        ),
        name="pick_heads",
    )(place, w_query, w_key, w_value)


def feed_kernel(place_ref, h_ref, cot_ref, w0_ref, w1_ref, wd_ref, hidden_ref, dg_ref, du_ref):
    high = h_ref.shape[0] // 2

    def run(wg_ref, wu_ref):
        for start in (0, high):
            rows = slice(start, start + high)
            gate = jnp.dot(h_ref[rows], wg_ref[...], preferred_element_type=F32)
            upper = jnp.dot(h_ref[rows], wu_ref[...], preferred_element_type=F32)
            gate_sig = jax.nn.sigmoid(gate)
            gate_act = gate * gate_sig
            hidden_ref[rows] = (gate_act * upper).astype(BF)
            d_hidden = lax.dot_general(
                cot_ref[rows], wd_ref[...], (((1,), (1,)), ((), ())), preferred_element_type=F32
            )
            d_gate = d_hidden * upper * (gate_sig + gate_act * (1.0 - gate_sig))
            dg_ref[rows] = d_gate.astype(BF)
            du_ref[rows] = (d_hidden * gate_act).astype(BF)

    even = place_ref[0] % 2 == 0

    @pl.when(even)
    def _():
        run(w0_ref, w1_ref)

    @pl.when(jnp.logical_not(even))
    def _():
        run(w1_ref, w0_ref)


def feed(place, h_all, cot_all, w0, w1, w_down, side):
    rows, width = h_all.shape
    units = w0.shape[1]
    block = min(256, units)
    steps = units // block
    full = pl.BlockSpec((rows, width), lambda j, place: (0, 0))
    columns = pl.BlockSpec((width, block), lambda j, place: (0, j))
    out = pl.BlockSpec((rows, block), lambda j, place: (0, j))
    return pl.pallas_call(
        feed_kernel,
        grid_spec=pltpu.PrefetchScalarGridSpec(
            num_scalar_prefetch=1,
            grid=(steps,),
            in_specs=[
                full,
                full,
                columns,
                columns,
                pl.BlockSpec(
                    (block, width), lambda j, place: ((place[1] + side) % 2 * steps + j, 0)
                ),
            ],
            out_specs=[out] * 3,
        ),
        out_shape=[jax.ShapeDtypeStruct((rows, units), BF)] * 3,
        compiler_params=pltpu.CompilerParams(vmem_limit_bytes=56 << 20),
        cost_estimate=cost(
            flops=6 * rows * width * units,
            transcendentals=rows * units,
            bytes_accessed=4 * rows * width + 6 * width * units + 6 * rows * units,
        ),
        name="feed",
    )(place, h_all, cot_all, w0, w1, w_down)


def unfeed(place, dg, du, w0, w1, first, last):
    high = last - first
    units = dg[0].shape[1]
    width = w0[0].shape[0]
    block = min(512, width)
    across = (((1,), (1,)), ((), ()))

    def kernel(place_ref, dg0, dg1, du0, du1, w00, w01, w10, w11, out_ref):
        def run(*pairs):
            total = None
            for d_ref, w_ref in pairs:
                part = lax.dot_general(
                    d_ref[...], w_ref[...], across, preferred_element_type=F32
                )
                total = part if total is None else total + part
            out_ref[...] = total.astype(BF)

        even = place_ref[0] % 2 == 0

        @pl.when(even)
        def _():
            run((dg0, w00), (du0, w10), (dg1, w01), (du1, w11))

        @pl.when(jnp.logical_not(even))
        def _():
            run((du0, w00), (dg0, w10), (du1, w01), (dg1, w11))

    return pl.pallas_call(
        kernel,
        grid_spec=pltpu.PrefetchScalarGridSpec(
            num_scalar_prefetch=1,
            grid=(width // block,),
            in_specs=[pl.BlockSpec((high, units), lambda n, place: (first // high, 0))] * 4
            + [pl.BlockSpec((block, units), lambda n, place: (n, 0))] * 4,
            out_specs=pl.BlockSpec((high, block), lambda n, place: (0, n)),
        ),
        out_shape=jax.ShapeDtypeStruct((high, width), BF),
        compiler_params=pltpu.CompilerParams(vmem_limit_bytes=48 << 20),
        cost_estimate=cost(
            flops=8 * high * units * width,
            transcendentals=0,
            bytes_accessed=8 * width * units + 8 * high * units + 2 * high * width,
        ),
        name="unfeed",
    )(place, *dg, *du, *w0, *w1)


def lower(place, hidden, w_down):
    rows, units = hidden[0].shape
    width = w_down.shape[1]
    block = min(512, width)

    def kernel(place_ref, h0, h1, w0, w1, out_ref):
        total = jnp.dot(h0[...], w0[...], preferred_element_type=F32)
        total = total + jnp.dot(h1[...], w1[...], preferred_element_type=F32)
        out_ref[...] = total.astype(BF)

    return pl.pallas_call(
        kernel,
        grid_spec=pltpu.PrefetchScalarGridSpec(
            num_scalar_prefetch=1,
            grid=(width // block,),
            in_specs=[pl.BlockSpec((rows, units), lambda n, place: (0, 0))] * 2
            + [
                pl.BlockSpec((units, block), lambda n, place: (place[1], n)),
                pl.BlockSpec((units, block), lambda n, place: (1 - place[1], n)),
            ],
            out_specs=pl.BlockSpec((rows, block), lambda n, place: (0, n)),
        ),
        out_shape=jax.ShapeDtypeStruct((rows, width), BF),
        compiler_params=pltpu.CompilerParams(vmem_limit_bytes=48 << 20),
        cost_estimate=cost(
            flops=4 * rows * units * width,
            transcendentals=0,
            bytes_accessed=4 * width * units + 4 * rows * units + 2 * rows * width,
        ),
        name="lower",
    )(place, *hidden, w_down, w_down)


def low_lanes(shape):
    return lax.broadcasted_iota(jnp.int32, shape, 1) < HEAD_DIM


def stack_heads(ref, group, upper):
    rows = []
    for head in range(0, GROUP, 2):
        start = (group * GROUP + head) * HEAD_DIM
        pair = ref[:, start : start + LANES].astype(F32)
        turned = pltpu.roll(pair, HEAD_DIM, 1)
        keep = low_lanes(pair.shape)
        if upper:
            keep = jnp.logical_not(keep)
            rows += [jnp.where(keep, turned, 0.0), jnp.where(keep, pair, 0.0)]
        else:
            rows += [jnp.where(keep, pair, 0.0), jnp.where(keep, turned, 0.0)]
    return jnp.concatenate(rows, 0).astype(BF)


def unstack_heads(stacked, ref, group, upper):
    span = ref.shape[0]
    for head in range(0, GROUP, 2):
        even = stacked[head * span : (head + 1) * span]
        odd = stacked[(head + 1) * span : (head + 2) * span]
        keep = low_lanes(even.shape)
        if upper:
            pair = jnp.where(keep, pltpu.roll(even, HEAD_DIM, 1), odd)
        else:
            pair = jnp.where(keep, even, pltpu.roll(odd, HEAD_DIM, 1))
        start = (group * GROUP + head) * HEAD_DIM
        ref[:, start : start + LANES] = pair.astype(ref.dtype)


def logits_of(place_ref, q_all, kv_own, kv_rest, span):
    own = lax.dot_general(q_all, kv_own, (((1,), (1,)), ((), ())), preferred_element_type=F32)
    rest = lax.dot_general(q_all, kv_rest, (((1,), (1,)), ((), ())), preferred_element_type=F32)
    row = lax.broadcasted_iota(jnp.int32, own.shape, 0) % span
    col = lax.broadcasted_iota(jnp.int32, own.shape, 1)
    own = jnp.where(col <= row, own, -1e30)
    depth = rest.shape[1] // span // 2 + 1
    block = lax.broadcasted_iota(jnp.int32, (1, rest.shape[1]), 1) // span + 1
    have = jnp.where(block == depth, place_ref[1], place_ref[0])
    need = jnp.where(block == depth, 1, block % depth)
    rest = rest + jnp.where(have >= need, 0.0, -1e30)
    return own, rest


def rest_of(kv_refs, cols):
    sibling = kv_refs[-1]
    parts = [ref[:, cols] for ref in kv_refs[1:-1]]
    parts += [sibling[i, :, cols] for i in range(sibling.shape[0])]
    return jnp.concatenate(parts, 0)


def attend_kernel(place_ref, q_ref, *refs):
    kv_refs = refs[:-2]
    out_ref, lse_ref = refs[-2:]
    span = q_ref.shape[0]
    for group in range(lse_ref.shape[1]):
        cols = slice(group * LANES, (group + 1) * LANES)
        q_all = stack_heads(q_ref, group, False)
        kv_own = kv_refs[0][:, cols]
        kv_rest = rest_of(kv_refs, cols)
        own, rest = logits_of(place_ref, q_all, kv_own, kv_rest, span)
        top = jnp.maximum(jnp.max(own, -1, keepdims=True), jnp.max(rest, -1, keepdims=True))
        own = jnp.exp(own - top)
        rest = jnp.exp(rest - top)
        total = jnp.sum(own, -1, keepdims=True) + jnp.sum(rest, -1, keepdims=True)
        out = jnp.dot(own.astype(BF), kv_own, preferred_element_type=F32)
        out = out + jnp.dot(rest.astype(BF), kv_rest, preferred_element_type=F32)
        unstack_heads(out / total, out_ref, group, True)
        lse_ref[0, group] = top + jnp.log(total)


def attend_back_kernel(place_ref, q_ref, do_ref, lse_ref, *refs):
    count = (len(refs) - 1) // 2
    kv_refs = refs[:count]
    dq_ref = refs[count]
    dkv_refs = refs[count + 1 :]
    span = q_ref.shape[0]
    flip = (((0,), (0,)), ((), ()))
    across = (((1,), (1,)), ((), ()))
    for group in range(lse_ref.shape[1]):
        cols = slice(group * LANES, (group + 1) * LANES)
        q_all = stack_heads(q_ref, group, False)
        do_all = stack_heads(do_ref, group, True)
        kv_own = kv_refs[0][:, cols]
        kv_rest = rest_of(kv_refs, cols)
        own, rest = logits_of(place_ref, q_all, kv_own, kv_rest, span)
        lse = lse_ref[0, group]
        own = jnp.exp(own - lse)
        rest = jnp.exp(rest - lse)
        d_own = lax.dot_general(do_all, kv_own, across, preferred_element_type=F32)
        d_rest = lax.dot_general(do_all, kv_rest, across, preferred_element_type=F32)
        inner = jnp.sum(own * d_own, -1, keepdims=True) + jnp.sum(rest * d_rest, -1, keepdims=True)
        d_own = (own * (d_own - inner)).astype(BF)
        d_rest = (rest * (d_rest - inner)).astype(BF)
        dq = jnp.dot(d_own, kv_own, preferred_element_type=F32)
        dq = dq + jnp.dot(d_rest, kv_rest, preferred_element_type=F32)
        unstack_heads(dq * HEAD_DIM**-0.5, dq_ref, group, False)
        dkv = lax.dot_general(d_own, q_all, flip, preferred_element_type=F32)
        dkv = dkv + lax.dot_general(own.astype(BF), do_all, flip, preferred_element_type=F32)
        dkv_refs[0][:, cols] = dkv.astype(BF)
        dkv = lax.dot_general(d_rest, q_all, flip, preferred_element_type=F32)
        dkv = dkv + lax.dot_general(rest.astype(BF), do_all, flip, preferred_element_type=F32)
        for i in range(count - 2):
            dkv_refs[i + 1][:, cols] = dkv[i * span : (i + 1) * span].astype(BF)
        for i in range(count - 1):
            start = (count - 2 + i) * span
            dkv_refs[-1][i, :, cols] = dkv[start : start + span].astype(BF)


def attend_specs(q_all, kv_all, span):
    depth, _, kv_width = kv_all[-1].shape
    groups = kv_width // LANES
    kv_spec = pl.BlockSpec((span, kv_width), lambda i, place: (i, 0))
    sibling = pl.BlockSpec((depth, span, kv_width), lambda i, place: (0, i, 0))
    return (
        pl.BlockSpec((span, q_all.shape[1]), lambda i, place: (i, 0)),
        [kv_spec] * depth + [sibling],
        pl.BlockSpec((1, groups, GROUP * span, 1), lambda i, place: (i, 0, 0, 0)),
        groups,
    )


def attend(place, q_all, kv_all, span):
    rows = q_all.shape[0]
    q_spec, kv_specs, lse_spec, groups = attend_specs(q_all, kv_all, span)
    cells = rows * groups * GROUP * span * (2 * len(kv_all) - 2)
    return pl.pallas_call(
        attend_kernel,
        grid_spec=pltpu.PrefetchScalarGridSpec(
            num_scalar_prefetch=1,
            grid=(rows // span,),
            in_specs=[q_spec] + kv_specs,
            out_specs=[q_spec, lse_spec],
        ),
        out_shape=(
            jax.ShapeDtypeStruct(q_all.shape, BF),
            jax.ShapeDtypeStruct((rows // span, groups, GROUP * span, 1), F32),
        ),
        compiler_params=pltpu.CompilerParams(vmem_limit_bytes=56 << 20),
        cost_estimate=cost(
            flops=2 * 4 * LANES * cells, transcendentals=cells, bytes_accessed=16 << 20
        ),
        name="attend",
    )(place, q_all, *kv_all)


def attend_back(place, q_all, do_all, lse, kv_all, span):
    rows = q_all.shape[0]
    q_spec, kv_specs, lse_spec, groups = attend_specs(q_all, kv_all, span)
    cells = rows * groups * GROUP * span * (2 * len(kv_all) - 2)
    outs = pl.pallas_call(
        attend_back_kernel,
        grid_spec=pltpu.PrefetchScalarGridSpec(
            num_scalar_prefetch=1,
            grid=(rows // span,),
            in_specs=[q_spec, q_spec, lse_spec] + kv_specs,
            out_specs=[q_spec] + kv_specs,
        ),
        out_shape=[jax.ShapeDtypeStruct(q_all.shape, BF)]
        + [jax.ShapeDtypeStruct(kv.shape, BF) for kv in kv_all],
        compiler_params=pltpu.CompilerParams(vmem_limit_bytes=60 << 20),
        cost_estimate=cost(
            flops=2 * 8 * LANES * cells, transcendentals=cells, bytes_accessed=24 << 20
        ),
        name="attend_back",
    )(place, q_all, do_all, lse, *kv_all)
    return outs[0], outs[1:]


def spread_kernel(place_ref, own_ref, other_ref, out_ref):
    @pl.when(pl.program_id(1) == 0)
    def _():
        out_ref[...] = own_ref[0].astype(F32)

    @pl.when(pl.program_id(1) == 1)
    def _():
        out_ref[...] = other_ref[0].astype(F32)


def spread(own, other, c, axis):
    count, high, wide = own.shape
    shape = {
        0: (high * 2 * count, wide),
        1: (high, wide * 2 * count),
        2: (high * 2, wide * count),
    }[axis]

    def out_place(i, side, place):
        core = (place[0] + side) % 2
        return [(2 * i + core, 0), (0, 2 * i + core), (core, i)][axis]

    return pl.pallas_call(
        spread_kernel,
        grid_spec=pltpu.PrefetchScalarGridSpec(
            num_scalar_prefetch=1,
            grid=(count, 2),
            in_specs=[pl.BlockSpec((1, high, wide), lambda i, side, place: (i, 0, 0))] * 2,
            out_specs=pl.BlockSpec((high, wide), out_place),
        ),
        out_shape=jax.ShapeDtypeStruct(shape, F32),
        compiler_params=pltpu.CompilerParams(vmem_limit_bytes=48 << 20),
        cost_estimate=cost(
            flops=own.size, transcendentals=0, bytes_accessed=12 * own.size
        ),
        name="spread",
    )(c.astype(jnp.int32)[None], own, other)


def dot(left, right):
    return jnp.dot(left, right, preferred_element_type=F32)


def dot_t(left, right):
    return lax.dot_general(left, right, (((1,), (1,)), ((), ())), preferred_element_type=F32)


def t_dot(left, right):
    return lax.dot_general(left, right, (((0,), (0,)), ((), ())), preferred_element_type=F32)


def exchange(field):
    return lax.all_to_all(field, "fsdp", split_axis=0, concat_axis=0, tiled=True)


def by_chunk(field, f):
    count = field.shape[0]
    return [lax.dynamic_index_in_dim(field, f ^ r, 0, keepdims=False) for r in range(count)]


def by_core(own, other, axis):
    first = lax.axis_index("core") == 0
    return jnp.stack([jnp.where(first, own, other), jnp.where(first, other, own)], axis)


def take(field, index, size, axis):
    return lax.dynamic_slice_in_dim(field, index * size, size, axis)


def body(
    tokens,
    positions,
    gain_attn,
    w_query,
    w_key,
    w_value,
    w_out,
    gain_ffn,
    w_gate,
    w_up,
    w_down,
    grad_out,
):
    seq_count, span, width = tokens.shape
    rows = seq_count * span
    count = lax.axis_size("fsdp")
    depth = lax.axis_size("zed")
    f = lax.axis_index("fsdp")
    z = lax.axis_index("zed")
    c = lax.axis_index("core")
    shard = width // count
    half_shard = shard // 2
    q_width = HEADS * HEAD_DIM // count
    k_width = KV_HEADS * HEAD_DIM // count
    kv_local = KV_HEADS // count
    ff = w_gate.shape[1]
    ff_half = ff // count // 2
    place = jnp.stack([z, c]).astype(jnp.int32)

    x_own = tokens.reshape(rows, width)
    x_list, _ = gather_rel(x_own)
    small = jnp.concatenate(
        [gain_attn.astype(F32), gain_ffn.astype(F32), positions.reshape(rows).astype(F32)]
    ).reshape(-1, LANES)
    small_list = [small] + [xor_send(small, r) for r in range(1, count)]
    gain_rows = shard // LANES

    def by_index(pieces):
        bit = 1
        while bit < count:
            odd = (f // bit) % 2 == 1
            pieces = [jnp.where(odd, pieces[i ^ bit], pieces[i]) for i in range(count)]
            bit *= 2
        return jnp.concatenate(pieces, 0)

    gain_one = by_index([piece[:gain_rows] for piece in small_list]).reshape(1, width)
    gain_two = by_index([piece[gain_rows : 2 * gain_rows] for piece in small_list]).reshape(
        1, width
    )
    places = jnp.concatenate([piece[2 * gain_rows :].reshape(rows) for piece in small_list])
    half_dim = HEAD_DIM // 2
    lane = jnp.arange(LANES, dtype=jnp.int32)
    freqs = jnp.exp((lane % half_dim).astype(F32) * (-2.0 * theta_log / (2 * half_dim)))
    angles = places[:, None] * freqs
    cos_tab = jnp.cos(angles)
    sin_tab = jnp.sin(angles) * jnp.where(lane % HEAD_DIM < half_dim, -1.0, 1.0)

    all_width = q_width + 2 * k_width
    w_own = exchange(pick_heads(place, w_query, w_key, w_value, count))
    w_other = core_swap(w_own)

    w0, x_list, cos_tab, sin_tab, gain_one = lax.optimization_barrier(
        (pick_units(place, w_gate, w_up, count), x_list, cos_tab, sin_tab, gain_one)
    )
    w0 = exchange(w0).reshape(width, ff_half)

    kv_width = 2 * k_width
    h_list, q_list, kv_list = [], [], []
    for r in range(count):
        piece = slice(r * rows, (r + 1) * rows)
        h, q, kv = project(
            place, x_list[r], gain_one, w_own, w_other, cos_tab[piece], sin_tab[piece], kv_width
        )
        h_list.append(h)
        q_list.append(q)
        kv_list.append(kv)
    h_all = jnp.concatenate(h_list, 0)
    q_all = jnp.concatenate(q_list, 0)
    stream = jnp.concatenate(kv_list, 0)
    kv_all = [stream]
    sibling = core_swap(stream)
    for step in range(1, depth):
        stream = z_up(stream)
        if step == 1:
            stream, w0 = lax.optimization_barrier((stream, w0))
        kv_all.append(stream)
    others = core_swap(jnp.stack(kv_all[1:]))
    kv_all = kv_all + [jnp.concatenate([sibling[None], others], 0)]
    w1, _ = lax.optimization_barrier((w0, stream))
    w1 = lax.ppermute(w1, "zed", [(i, i ^ 1) for i in range(depth)])
    cot_own = grad_out.reshape(rows, width)
    cot_abs, _ = lax.optimization_barrier((cot_own, w0))
    cot_abs = lax.all_gather(cot_abs, "fsdp", axis=0, tiled=True)
    attended, lse = attend(place, q_all, kv_all, span)
    w0 = [w0, core_swap(w0)]
    attended, cot_abs, w0 = lax.optimization_barrier((attended, cot_abs, w0))


    def chunk(field, r):
        return field[r * rows : (r + 1) * rows]

    branch = [dot(chunk(attended, r), w_out) for r in range(count)]
    branch = reduce_rel([branch[0]] + [part.astype(BF) for part in branch[1:]])
    cot_all = jnp.concatenate([take(cot_abs, f ^ r, rows, 0) for r in range(count)], 0)
    branch, cot_all = lax.optimization_barrier((branch, cot_all))
    x_float = x_own.astype(F32)
    resid = x_float + branch
    inv_two = lax.rsqrt(jnp.mean(resid * resid, -1, keepdims=True) + norm_eps)
    resid_hat = resid * inv_two
    h2_list, w1 = gather_rel((resid_hat * gain_two).astype(BF), w1)
    h2_all = jnp.concatenate(h2_list, 0)
    w1 = [w1, core_swap(w1)]

    def summed(left, right):
        other = core_swap(t_dot(left, right[1]).astype(BF))
        return (t_dot(left, right[0]) + other.astype(F32)).astype(BF)

    cut = width // 2
    fed = [None, feed(place, h2_all, cot_all, w0[1], w1[1], w_down, 1)]
    h2_late, fed[1] = lax.optimization_barrier((h2_all, fed[1]))
    fed[0] = feed(place, h2_late, cot_all, w0[0], w1[0], w_down, 0)
    hidden, d_gate, d_up = zip(*fed)
    gate0 = summed(h2_all[:, :cut], d_gate)
    gate0, d_gate, d_up = lax.optimization_barrier((gate0, d_gate, d_up))
    middle = count // 2 * rows
    far = unfeed(place, d_gate, d_up, w0, w1, middle, count * rows)
    near = unfeed(place, d_gate, d_up, w0, w1, 0, middle)

    def core_sum(own, other):
        return add_low(own, core_swap(other))

    near, late = lax.optimization_barrier((near, (h2_all, hidden, cot_all)))
    d_h2 = reduce_rel([chunk(part, r) for part in (near, far) for r in range(count // 2)])
    down = lower(place, hidden, w_down)
    line = Line()
    h2_late, hidden_late, cot_late = late
    gate1 = summed(h2_late[:, cut:], d_gate)
    d_h2, down = line.round((d_h2, down), gate0=gate0)
    up_sum = summed(h2_late, d_up)
    up_parts = [up_sum[:cut], up_sum[cut:]]
    down_part = core_sum(*[t_dot(hidden_late[side], cot_late).astype(BF) for side in range(2)])

    d_hat_two = d_h2 * gain_two
    part_gain_two = jnp.sum(d_h2 * resid_hat, 0)
    d_resid = cot_own.astype(F32) + inv_two * (
        d_hat_two - resid_hat * jnp.mean(d_hat_two * resid_hat, -1, keepdims=True)
    )
    d_branch, _ = gather_rel(d_resid.astype(BF))
    d_branch = line.round(d_branch, gate1=gate1)
    d_branch = jnp.concatenate(d_branch, 0)
    d_attended = dot_t(d_branch, w_out).astype(BF)
    dq, dkv_all = attend_back(place, q_all, d_attended, lse, kv_all, span)
    dq, dkv_all, down = line.round((dq, dkv_all, down), up0=up_parts[0])
    d_q = unrotate(dq, cos_tab, sin_tab, rows)
    up_last = up_parts[1]
    tail = None
    from_sibling = core_swap(dkv_all[-1])
    for step in reversed(range(depth)):
        here = dkv_all[step].astype(F32) + from_sibling[step].astype(F32)
        if tail is not None:
            moved = z_down(tail)
            if step == depth - 2:
                moved, up_last = line.hold((moved, up_last))
            here = here + moved.astype(F32)
        tail = here.astype(BF)
    down = reduce_rel([chunk(down, r) for r in range(count)])
    layer_out = (resid + down).astype(BF).reshape(seq_count, span, width)
    tail, layer_out = line.round((tail, layer_out), up1=up_last)
    def row_pair(field):
        field = field.astype(BF).reshape(count, 2, half_shard, -1)
        own = lax.dynamic_index_in_dim(field, c, 1, keepdims=False)
        other = lax.dynamic_index_in_dim(field, 1 - c, 1, keepdims=False)
        return own, other

    g_q = row_pair(t_dot(h_all, d_q))
    d_branch, _ = lax.optimization_barrier((d_branch, d_q))
    g_out = t_dot(attended, d_branch).astype(BF)
    out_half = q_width // 2
    g_out = (take(g_out, c, out_half, 0), take(g_out, 1 - c, out_half, 0))
    g_qo = core_sum(
        *[
            jnp.concatenate([q.reshape(-1, q_width), out.reshape(-1, q_width)], 0)
            for q, out in zip(g_q, g_out)
        ]
    )
    d_kv, d_h1_all = unproject(place, d_q, tail, w_own, w_other, cos_tab, sin_tab)
    d_h1 = reduce_rel([chunk(d_h1_all, r) for r in range(count)])
    g_kv = core_sum(*row_pair(t_dot(h_all, d_kv)))
    d_h1, g_kv = line.round((d_h1, g_kv), qo=g_qo)

    inv_one = lax.rsqrt(jnp.mean(x_float * x_float, -1, keepdims=True) + norm_eps)
    x_hat = x_float * inv_one
    d_hat_one = d_h1 * gain_one
    part_gain_one = jnp.sum(d_h1 * x_hat, 0)
    d_input = d_resid + inv_one * (
        d_hat_one - x_hat * jnp.mean(d_hat_one * x_hat, -1, keepdims=True)
    )
    grad_tokens = d_input.astype(BF).reshape(seq_count, span, width)
    gains = jnp.stack([part_gain_one, part_gain_two], 1)
    gains = jnp.pad(gains, ((0, 0), (0, LANES - 2)))
    gains = reduce_rel(by_chunk(gains.astype(BF).reshape(count, shard, LANES), f))
    gains = gains.astype(BF)
    gains = core_sum(take(gains, c, half_shard, 0), take(gains, 1 - c, half_shard, 0))

    def pair_rows(own):
        return spread(own[None], core_swap(own)[None], c, 0)

    def to_rows(own):
        own = exchange(own.reshape(count, shard, ff_half))
        return spread(own, core_swap(own), c, 1)

    cut = ff_half // 2
    gains = line.round(gains, kv=g_kv, down0=down_part[:cut])

    def whole(name):
        return jnp.concatenate(line.take(name + "0", name + "1"), 0)

    grad_gate = to_rows(whole("gate"))
    grad_gate = line.round(grad_gate, gains=gains, down1=down_part[cut:])
    grad_up = to_rows(whole("up"))
    (g_qo,) = line.take("qo")
    high = count * half_shard
    grad_out_w = pair_rows(g_qo[high:].reshape(out_half, width))
    g_q = exchange(g_qo[:high].reshape(count, half_shard, q_width))
    grad_q = spread(g_q, core_swap(g_q), c, 2)
    grad_up, grad_out_w, grad_q = line.round((grad_up, grad_out_w, grad_q))
    (g_kv,) = line.take("kv")
    g_kv = exchange(g_kv)
    g_kv = by_core(g_kv, core_swap(g_kv), 0).astype(F32)
    g_kv = jnp.transpose(g_kv, (0, 2, 1, 3)).reshape(shard, count * kv_local, 2, HEAD_DIM)
    grad_k = g_kv[:, :, 0].reshape(shard, count * k_width)
    grad_v = g_kv[:, :, 1].reshape(shard, count * k_width)
    grad_k, grad_v = line.round((grad_k, grad_v))
    (gains,) = line.take("gains")
    gains = by_core(gains, core_swap(gains), 0).astype(F32).reshape(shard, LANES)
    grad_down = pair_rows(whole("down"))
    return (
        layer_out,
        grad_tokens,
        gains[:, 0],
        grad_q,
        grad_k,
        grad_v,
        grad_out_w,
        gains[:, 1],
        grad_gate,
        grad_up,
        grad_down,
    )


def solution(mesh):
    fsdp, seq = mesh.devices.shape
    split = Mesh(mesh.devices.reshape(fsdp, seq // 2, 2), ("fsdp", "zed", "core"))
    field = P("fsdp", ("zed", "core"), None)
    vector = P("fsdp")
    matrix = P("fsdp", None)
    return jax.shard_map(
        body,
        mesh=split,
        in_specs=(
            field,
            P("fsdp", ("zed", "core")),
            vector,
            matrix,
            matrix,
            matrix,
            matrix,
            vector,
            matrix,
            matrix,
            matrix,
            field,
        ),
        out_specs=(
            field,
            field,
            vector,
            matrix,
            matrix,
            matrix,
            matrix,
            vector,
            matrix,
            matrix,
            matrix,
        ),
        check_vma=False,
    )
```

```python
import functools
import math

import jax
import jax.numpy as jnp
import numpy as np
from jax import lax
from jax.experimental import pallas as pl
from jax.experimental.pallas import tpu as pltpu
from jax.sharding import Mesh
from jax.sharding import PartitionSpec as P

HEADS = 32
KV_HEADS = 8
HEAD_DIM = 64
GROUP = HEADS // KV_HEADS
LANES = 128

norm_eps = 1e-05
theta_log = math.log(500000.0)
BF = jnp.bfloat16
F32 = jnp.float32


def xor_send(field, bit):
    count = lax.axis_size("fsdp")
    return lax.ppermute(field, "fsdp", [(i, i ^ bit) for i in range(count)])


def core_swap(field):
    return lax.ppermute(field, "core", [(0, 1), (1, 0)])


def gather_rel(own, tie=()):
    count = lax.axis_size("fsdp")
    chunks = [own, xor_send(own, 1)]
    if count == 4:
        chunks.append(xor_send(own, 2))
    chunks, tie = lax.optimization_barrier((chunks, tie))
    if count == 4:
        half = own.shape[0] // 2
        top = xor_send(chunks[1][:half], 2)
        low = xor_send(chunks[2][half:], 1)
        return chunks + [jnp.concatenate([top, low], 0)], tie
    bit = 2
    while bit < count:
        chunks = chunks + [xor_send(chunk, bit) for chunk in chunks]
        bit *= 2
    return chunks, tie


def reduce_rel(partials):
    count = lax.axis_size("fsdp")
    if count == 4:
        zero, one, two, three = partials
        half = three.shape[0] // 2
        top = xor_send(three[:half], 1)
        low = xor_send(three[half:], 2)
        two = jnp.concatenate([add_low(two[:half], top), two[half:]], 0)
        one = jnp.concatenate([one[:half], add_low(one[half:], low)], 0)
        one = xor_send(one, 1)
        two = xor_send(two, 2)
        return zero.astype(F32) + one.astype(F32) + two.astype(F32)
    chunks = list(partials)
    bit = count // 2
    while bit >= 1:
        sent = [xor_send(chunks[bit + i].astype(BF), bit) for i in range(bit)]
        chunks = [chunks[i].astype(F32) + sent[i].astype(F32) for i in range(bit)]
        bit //= 2
    return chunks[0]


def add_low(left, right):
    return (left.astype(F32) + right.astype(F32)).astype(BF)


def z_steps():
    count = lax.axis_size("zed")
    half = count // 2
    inwards = [[(i, i + 1), (count - 1 - i, count - 2 - i)] for i in range(half - 1)]
    outwards = [[(b, a) for a, b in pairs] for pairs in reversed(inwards)]
    middle = [(half - 1, half), (half, half - 1)]
    return [(pairs, True) for pairs in inwards + [middle]] + [(pairs, False) for pairs in outwards]


def z_move(field, stage):
    return lax.ppermute(field, "zed", z_steps()[stage][0])


def z_join(field, moved, stage):
    pairs, adds = z_steps()[stage]
    if adds:
        return add_low(field, moved)
    place = lax.axis_index("zed")
    return jnp.where((place == pairs[0][1]) | (place == pairs[1][1]), moved, field)


class Line:
    def __init__(self):
        self.last = len(z_steps())
        self.running = []
        self.ready = {}

    def round(self, tie, **fields):
        self.running += [(name, 0, field) for name, field in fields.items()]
        moved = [z_move(field, stage) for _, stage, field in self.running]
        tie, moved = lax.optimization_barrier((tie, moved))
        left = []
        for (name, stage, field), arrived in zip(self.running, moved):
            field = z_join(field, arrived, stage)
            if stage + 1 == self.last:
                self.ready[name] = field
            else:
                left.append((name, stage + 1, field))
        self.running = left
        return tie

    def take(self, *names):
        while not all(name in self.ready for name in names):
            self.round(())
        return [self.ready[name] for name in names]

    def hold(self, tie):
        held = [field for _, _, field in self.running]
        tie, held = lax.optimization_barrier((tie, held))
        self.running = [(name, stage, h) for (name, stage, _), h in zip(self.running, held)]
        return tie


def z_up(field):
    count = lax.axis_size("zed")
    return lax.ppermute(field, "zed", [(i, i + 1) for i in range(count - 1)])


def z_down(field):
    count = lax.axis_size("zed")
    return lax.ppermute(field, "zed", [(i + 1, i) for i in range(count - 1)])


def cost(flops, transcendentals, bytes_accessed):
    return pl.CostEstimate(
        flops=flops // 32, transcendentals=transcendentals // 32, bytes_accessed=bytes_accessed // 32
    )


def rotated(field, cos_tab, sin_tab):
    lane = lax.broadcasted_iota(jnp.int32, field.shape, 1)
    other = jnp.where(
        lane % HEAD_DIM < HEAD_DIM // 2,
        pltpu.roll(field, LANES - HEAD_DIM // 2, 1),
        pltpu.roll(field, HEAD_DIM // 2, 1),
    )
    return field * cos_tab + other * sin_tab


def kv_tables(cos_tab, sin_tab):
    lane = lax.broadcasted_iota(jnp.int32, cos_tab.shape, 1)
    return (
        jnp.where(lane < HEAD_DIM, cos_tab, 1.0),
        jnp.where(lane < HEAD_DIM, sin_tab, 0.0),
    )


def block_lanes(i, core, shard):
    half = shard // 2
    return pl.ds(pl.multiple_of(i * shard + core * half, half), half)


def project_kernel(
    place_ref, x_ref, gain_ref, own_ref, other_ref, cos_ref, sin_ref, h_ref, q_ref, kv_ref
):
    x = x_ref[...].astype(F32)
    inv = lax.rsqrt(jnp.mean(x * x, -1, keepdims=True) + norm_eps)
    h_ref[...] = (x * inv * gain_ref[...]).astype(BF)
    cos_tab = cos_ref[...]
    sin_tab = sin_ref[...]
    kv_cos, kv_sin = kv_tables(cos_tab, sin_tab)
    core = place_ref[1]
    raw = jnp.zeros((x.shape[0], own_ref.shape[2]), F32)
    for i in range(own_ref.shape[0]):
        for ref, side in ((own_ref, core), (other_ref, 1 - core)):
            cols = block_lanes(i, side, 2 * own_ref.shape[1])
            raw = raw + jnp.dot(h_ref[:, cols], ref[i], preferred_element_type=F32)
    q_width = q_ref.shape[1]
    for start in range(0, q_width, LANES):
        part = rotated(raw[:, start : start + LANES], cos_tab, sin_tab)
        q_ref[:, start : start + LANES] = (part * HEAD_DIM**-0.5).astype(BF)
    for start in range(0, kv_ref.shape[1], LANES):
        part = rotated(raw[:, q_width + start : q_width + start + LANES], kv_cos, kv_sin)
        kv_ref[:, start : start + LANES] = part.astype(BF)


def project(place, x, gain, w_own, w_other, cos_tab, sin_tab, kv_width):
    rows, width = x.shape
    all_width = w_own.shape[2]
    q_width = all_width - kv_width
    return pl.pallas_call(
        project_kernel,
        in_specs=[pl.BlockSpec(memory_space=pltpu.SMEM)]
        + [pl.BlockSpec(memory_space=pltpu.VMEM)] * 6,
        out_shape=(
            jax.ShapeDtypeStruct((rows, width), BF),
            jax.ShapeDtypeStruct((rows, q_width), BF),
            jax.ShapeDtypeStruct((rows, kv_width), BF),
        ),
        compiler_params=pltpu.CompilerParams(vmem_limit_bytes=40 << 20),
        cost_estimate=cost(
            flops=2 * rows * width * all_width,
            transcendentals=rows,
            bytes_accessed=4 * rows * width + 2 * width * all_width,
        ),
        name="project",
    )(place, x, gain, w_own, w_other, cos_tab, sin_tab)


def unrotate_kernel(dq_ref, cos_ref, sin_ref, d_ref):
    for start in range(0, dq_ref.shape[1], LANES):
        part = dq_ref[:, start : start + LANES].astype(F32)
        d_ref[:, start : start + LANES] = rotated(part, cos_ref[...], -sin_ref[...]).astype(BF)


def unrotate(dq, cos_tab, sin_tab, block):
    rows, wide = dq.shape
    tables = pl.BlockSpec((block, LANES), lambda i: (i, 0))
    field = pl.BlockSpec((block, wide), lambda i: (i, 0))
    return pl.pallas_call(
        unrotate_kernel,
        grid=(rows // block,),
        in_specs=[field, tables, tables],
        out_specs=field,
        out_shape=jax.ShapeDtypeStruct(dq.shape, BF),
        cost_estimate=cost(
            flops=6 * rows * wide, transcendentals=0, bytes_accessed=6 * rows * wide
        ),
        name="unrotate",
    )(dq, cos_tab, sin_tab)


def unproject_kernel(
    place_ref, dq_ref, dkv_ref, own_ref, other_ref, cos_ref, sin_ref, d_ref, dh_ref
):
    kv_cos, kv_sin = kv_tables(cos_ref[...], -sin_ref[...])
    q_width = dq_ref.shape[1]
    for start in range(0, dkv_ref.shape[1], LANES):
        part = rotated(dkv_ref[:, start : start + LANES].astype(F32), kv_cos, kv_sin)
        d_ref[:, start : start + LANES] = part.astype(BF)
    core = place_ref[1]
    across = (((1,), (1,)), ((), ()))
    for i in range(own_ref.shape[0]):
        for ref, side in ((own_ref, core), (other_ref, 1 - core)):
            cols = block_lanes(i, side, 2 * own_ref.shape[1])
            total = lax.dot_general(
                dq_ref[...], ref[i, :, :q_width], across, preferred_element_type=F32
            )
            total = total + lax.dot_general(
                d_ref[...], ref[i, :, q_width:], across, preferred_element_type=F32
            )
            dh_ref[:, cols] = total.astype(BF)


def unproject(place, dq, dkv, w_own, w_other, cos_tab, sin_tab):
    rows = dq.shape[0]
    count, half, cols = w_own.shape
    width = 2 * count * half
    block = rows // count

    def row_block(wide):
        return pl.BlockSpec((block, wide), lambda i, place: (i, 0))

    weights = pl.BlockSpec(w_own.shape, lambda i, place: (0, 0, 0))
    return pl.pallas_call(
        unproject_kernel,
        grid_spec=pltpu.PrefetchScalarGridSpec(
            num_scalar_prefetch=1,
            grid=(rows // block,),
            in_specs=[
                row_block(dq.shape[1]),
                row_block(dkv.shape[1]),
                weights,
                weights,
                row_block(LANES),
                row_block(LANES),
            ],
            out_specs=(row_block(dkv.shape[1]), row_block(width)),
        ),
        out_shape=(
            jax.ShapeDtypeStruct(dkv.shape, BF),
            jax.ShapeDtypeStruct((rows, width), BF),
        ),
        compiler_params=pltpu.CompilerParams(vmem_limit_bytes=40 << 20),
        cost_estimate=cost(
            flops=2 * rows * width * cols,
            transcendentals=0,
            bytes_accessed=2 * rows * width + 2 * width * cols + 4 * rows * cols,
        ),
        name="unproject",
    )(place, dq, dkv, w_own, w_other, cos_tab, sin_tab)


def pick_units(place, w_even, w_odd, count):
    high, wide = w_even.shape
    units = wide // count // 2

    def kernel(place_ref, even_ref, odd_ref, out_ref):
        even = place_ref[0] % 2 == 0

        @pl.when(even)
        def _():
            out_ref[0] = even_ref[...]

        @pl.when(jnp.logical_not(even))
        def _():
            out_ref[0] = odd_ref[...]

    def columns(parity):
        def index(i, place):
            here = place[0] % 2 == parity
            return (0, jnp.where(here, 2 * i + place[1], 0))

        return pl.BlockSpec((high, units), index)

    return pl.pallas_call(
        kernel,
        grid_spec=pltpu.PrefetchScalarGridSpec(
            num_scalar_prefetch=1,
            grid=(count,),
            in_specs=[columns(0), columns(1)],
            out_specs=pl.BlockSpec((1, high, units), lambda i, place: (i, 0, 0)),
        ),
        out_shape=jax.ShapeDtypeStruct((count, high, units), BF),
        cost_estimate=cost(
            flops=0, transcendentals=0, bytes_accessed=4 * count * high * units
        ),
        name="pick_units",
    )(place, w_even, w_odd)


def pick_heads(place, w_query, w_key, w_value, count):
    high = w_query.shape[0] // 2
    q_width = w_query.shape[1] // count
    k_width = w_key.shape[1] // count

    def kernel(place_ref, q_ref, k_ref, v_ref, out_ref):
        for i in range(count):
            out_ref[i, :, :q_width] = q_ref[:, i * q_width : (i + 1) * q_width]
            for head in range(k_width // HEAD_DIM):
                cols = slice(i * k_width + head * HEAD_DIM, i * k_width + (head + 1) * HEAD_DIM)
                start = q_width + head * LANES
                out_ref[i, :, start : start + LANES] = jnp.concatenate(
                    [k_ref[:, cols], v_ref[:, cols]], 1
                )

    def half(weight):
        return pl.BlockSpec((high, weight.shape[1]), lambda i, place: (place[1], 0))

    all_width = q_width + 2 * k_width
    return pl.pallas_call(
        kernel,
        grid_spec=pltpu.PrefetchScalarGridSpec(
            num_scalar_prefetch=1,
            grid=(1,),
            in_specs=[half(w_query), half(w_key), half(w_value)],
            out_specs=pl.BlockSpec((count, high, all_width), lambda i, place: (0, 0, 0)),
        ),
        out_shape=jax.ShapeDtypeStruct((count, high, all_width), BF),
        cost_estimate=cost(
            flops=0, transcendentals=0, bytes_accessed=4 * count * high * all_width
        ),
        name="pick_heads",
    )(place, w_query, w_key, w_value)


def feed_kernel(place_ref, h_ref, cot_ref, w0_ref, w1_ref, wd_ref, hidden_ref, dg_ref, du_ref):
    high = h_ref.shape[0] // 2

    def run(wg_ref, wu_ref):
        for start in (0, high):
            rows = slice(start, start + high)
            gate = jnp.dot(h_ref[rows], wg_ref[...], preferred_element_type=F32)
            upper = jnp.dot(h_ref[rows], wu_ref[...], preferred_element_type=F32)
            gate_sig = jax.nn.sigmoid(gate)
            gate_act = gate * gate_sig
            hidden_ref[rows] = (gate_act * upper).astype(BF)
            d_hidden = lax.dot_general(
                cot_ref[rows], wd_ref[...], (((1,), (1,)), ((), ())), preferred_element_type=F32
            )
            d_gate = d_hidden * upper * (gate_sig + gate_act * (1.0 - gate_sig))
            dg_ref[rows] = d_gate.astype(BF)
            du_ref[rows] = (d_hidden * gate_act).astype(BF)

    even = place_ref[0] % 2 == 0

    @pl.when(even)
    def _():
        run(w0_ref, w1_ref)

    @pl.when(jnp.logical_not(even))
    def _():
        run(w1_ref, w0_ref)


def feed(place, h_all, cot_all, w0, w1, w_down, side):
    rows, width = h_all.shape
    units = w0.shape[1]
    block = min(256, units)
    steps = units // block
    full = pl.BlockSpec((rows, width), lambda j, place: (0, 0))
    columns = pl.BlockSpec((width, block), lambda j, place: (0, j))
    out = pl.BlockSpec((rows, block), lambda j, place: (0, j))
    return pl.pallas_call(
        feed_kernel,
        grid_spec=pltpu.PrefetchScalarGridSpec(
            num_scalar_prefetch=1,
            grid=(steps,),
            in_specs=[
                full,
                full,
                columns,
                columns,
                pl.BlockSpec(
                    (block, width), lambda j, place: ((place[1] + side) % 2 * steps + j, 0)
                ),
            ],
            out_specs=[out] * 3,
        ),
        out_shape=[jax.ShapeDtypeStruct((rows, units), BF)] * 3,
        compiler_params=pltpu.CompilerParams(vmem_limit_bytes=56 << 20),
        cost_estimate=cost(
            flops=6 * rows * width * units,
            transcendentals=rows * units,
            bytes_accessed=4 * rows * width + 6 * width * units + 6 * rows * units,
        ),
        name="feed",
    )(place, h_all, cot_all, w0, w1, w_down)


def unfeed(place, dg, du, w0, w1, first, last):
    high = last - first
    units = dg[0].shape[1]
    width = w0[0].shape[0]
    block = min(512, width)
    across = (((1,), (1,)), ((), ()))

    def kernel(place_ref, dg0, dg1, du0, du1, w00, w01, w10, w11, out_ref):
        def run(*pairs):
            total = None
            for d_ref, w_ref in pairs:
                part = lax.dot_general(
                    d_ref[...], w_ref[...], across, preferred_element_type=F32
                )
                total = part if total is None else total + part
            out_ref[...] = total.astype(BF)

        even = place_ref[0] % 2 == 0

        @pl.when(even)
        def _():
            run((dg0, w00), (du0, w10), (dg1, w01), (du1, w11))

        @pl.when(jnp.logical_not(even))
        def _():
            run((du0, w00), (dg0, w10), (du1, w01), (dg1, w11))

    return pl.pallas_call(
        kernel,
        grid_spec=pltpu.PrefetchScalarGridSpec(
            num_scalar_prefetch=1,
            grid=(width // block,),
            in_specs=[pl.BlockSpec((high, units), lambda n, place: (first // high, 0))] * 4
            + [pl.BlockSpec((block, units), lambda n, place: (n, 0))] * 4,
            out_specs=pl.BlockSpec((high, block), lambda n, place: (0, n)),
        ),
        out_shape=jax.ShapeDtypeStruct((high, width), BF),
        compiler_params=pltpu.CompilerParams(vmem_limit_bytes=48 << 20),
        cost_estimate=cost(
            flops=8 * high * units * width,
            transcendentals=0,
            bytes_accessed=8 * width * units + 8 * high * units + 2 * high * width,
        ),
        name="unfeed",
    )(place, *dg, *du, *w0, *w1)


def lower(place, hidden, w_down):
    rows, units = hidden[0].shape
    width = w_down.shape[1]
    block = min(512, width)

    def kernel(place_ref, h0, h1, w0, w1, out_ref):
        total = jnp.dot(h0[...], w0[...], preferred_element_type=F32)
        total = total + jnp.dot(h1[...], w1[...], preferred_element_type=F32)
        out_ref[...] = total.astype(BF)

    return pl.pallas_call(
        kernel,
        grid_spec=pltpu.PrefetchScalarGridSpec(
            num_scalar_prefetch=1,
            grid=(width // block,),
            in_specs=[pl.BlockSpec((rows, units), lambda n, place: (0, 0))] * 2
            + [
                pl.BlockSpec((units, block), lambda n, place: (place[1], n)),
                pl.BlockSpec((units, block), lambda n, place: (1 - place[1], n)),
            ],
            out_specs=pl.BlockSpec((rows, block), lambda n, place: (0, n)),
        ),
        out_shape=jax.ShapeDtypeStruct((rows, width), BF),
        compiler_params=pltpu.CompilerParams(vmem_limit_bytes=48 << 20),
        cost_estimate=cost(
            flops=4 * rows * units * width,
            transcendentals=0,
            bytes_accessed=4 * width * units + 4 * rows * units + 2 * rows * width,
        ),
        name="lower",
    )(place, *hidden, w_down, w_down)


def low_lanes(shape):
    return lax.broadcasted_iota(jnp.int32, shape, 1) < HEAD_DIM


def stack_heads(ref, group, upper):
    rows = []
    for head in range(0, GROUP, 2):
        start = (group * GROUP + head) * HEAD_DIM
        pair = ref[:, start : start + LANES].astype(F32)
        turned = pltpu.roll(pair, HEAD_DIM, 1)
        keep = low_lanes(pair.shape)
        if upper:
            keep = jnp.logical_not(keep)
            rows += [jnp.where(keep, turned, 0.0), jnp.where(keep, pair, 0.0)]
        else:
            rows += [jnp.where(keep, pair, 0.0), jnp.where(keep, turned, 0.0)]
    return jnp.concatenate(rows, 0).astype(BF)


def unstack_heads(stacked, ref, group, upper):
    span = ref.shape[0]
    for head in range(0, GROUP, 2):
        even = stacked[head * span : (head + 1) * span]
        odd = stacked[(head + 1) * span : (head + 2) * span]
        keep = low_lanes(even.shape)
        if upper:
            pair = jnp.where(keep, pltpu.roll(even, HEAD_DIM, 1), odd)
        else:
            pair = jnp.where(keep, even, pltpu.roll(odd, HEAD_DIM, 1))
        start = (group * GROUP + head) * HEAD_DIM
        ref[:, start : start + LANES] = pair.astype(ref.dtype)


def logits_of(place_ref, q_all, kv_own, kv_rest, span):
    own = lax.dot_general(q_all, kv_own, (((1,), (1,)), ((), ())), preferred_element_type=F32)
    rest = lax.dot_general(q_all, kv_rest, (((1,), (1,)), ((), ())), preferred_element_type=F32)
    row = lax.broadcasted_iota(jnp.int32, own.shape, 0) % span
    col = lax.broadcasted_iota(jnp.int32, own.shape, 1)
    own = jnp.where(col <= row, own, -1e30)
    depth = rest.shape[1] // span // 2 + 1
    block = lax.broadcasted_iota(jnp.int32, (1, rest.shape[1]), 1) // span + 1
    have = jnp.where(block == depth, place_ref[1], place_ref[0])
    need = jnp.where(block == depth, 1, block % depth)
    rest = rest + jnp.where(have >= need, 0.0, -1e30)
    return own, rest


def rest_of(kv_refs, cols):
    sibling = kv_refs[-1]
    parts = [ref[:, cols] for ref in kv_refs[1:-1]]
    parts += [sibling[i, :, cols] for i in range(sibling.shape[0])]
    return jnp.concatenate(parts, 0)


def attend_kernel(place_ref, q_ref, *refs):
    kv_refs = refs[:-2]
    out_ref, lse_ref = refs[-2:]
    span = q_ref.shape[0]
    for group in range(lse_ref.shape[1]):
        cols = slice(group * LANES, (group + 1) * LANES)
        q_all = stack_heads(q_ref, group, False)
        kv_own = kv_refs[0][:, cols]
        kv_rest = rest_of(kv_refs, cols)
        own, rest = logits_of(place_ref, q_all, kv_own, kv_rest, span)
        top = jnp.maximum(jnp.max(own, -1, keepdims=True), jnp.max(rest, -1, keepdims=True))
        own = jnp.exp(own - top)
        rest = jnp.exp(rest - top)
        total = jnp.sum(own, -1, keepdims=True) + jnp.sum(rest, -1, keepdims=True)
        out = jnp.dot(own.astype(BF), kv_own, preferred_element_type=F32)
        out = out + jnp.dot(rest.astype(BF), kv_rest, preferred_element_type=F32)
        unstack_heads(out / total, out_ref, group, True)
        lse_ref[0, group] = top + jnp.log(total)


def attend_back_kernel(place_ref, q_ref, do_ref, lse_ref, *refs):
    count = (len(refs) - 1) // 2
    kv_refs = refs[:count]
    dq_ref = refs[count]
    dkv_refs = refs[count + 1 :]
    span = q_ref.shape[0]
    flip = (((0,), (0,)), ((), ()))
    across = (((1,), (1,)), ((), ()))
    for group in range(lse_ref.shape[1]):
        cols = slice(group * LANES, (group + 1) * LANES)
        q_all = stack_heads(q_ref, group, False)
        do_all = stack_heads(do_ref, group, True)
        kv_own = kv_refs[0][:, cols]
        kv_rest = rest_of(kv_refs, cols)
        own, rest = logits_of(place_ref, q_all, kv_own, kv_rest, span)
        lse = lse_ref[0, group]
        own = jnp.exp(own - lse)
        rest = jnp.exp(rest - lse)
        d_own = lax.dot_general(do_all, kv_own, across, preferred_element_type=F32)
        d_rest = lax.dot_general(do_all, kv_rest, across, preferred_element_type=F32)
        inner = jnp.sum(own * d_own, -1, keepdims=True) + jnp.sum(rest * d_rest, -1, keepdims=True)
        d_own = (own * (d_own - inner)).astype(BF)
        d_rest = (rest * (d_rest - inner)).astype(BF)
        dq = jnp.dot(d_own, kv_own, preferred_element_type=F32)
        dq = dq + jnp.dot(d_rest, kv_rest, preferred_element_type=F32)
        unstack_heads(dq * HEAD_DIM**-0.5, dq_ref, group, False)
        dkv = lax.dot_general(d_own, q_all, flip, preferred_element_type=F32)
        dkv = dkv + lax.dot_general(own.astype(BF), do_all, flip, preferred_element_type=F32)
        dkv_refs[0][:, cols] = dkv.astype(BF)
        dkv = lax.dot_general(d_rest, q_all, flip, preferred_element_type=F32)
        dkv = dkv + lax.dot_general(rest.astype(BF), do_all, flip, preferred_element_type=F32)
        for i in range(count - 2):
            dkv_refs[i + 1][:, cols] = dkv[i * span : (i + 1) * span].astype(BF)
        for i in range(count - 1):
            start = (count - 2 + i) * span
            dkv_refs[-1][i, :, cols] = dkv[start : start + span].astype(BF)


def attend_specs(q_all, kv_all, span):
    depth, _, kv_width = kv_all[-1].shape
    groups = kv_width // LANES
    kv_spec = pl.BlockSpec((span, kv_width), lambda i, place: (i, 0))
    sibling = pl.BlockSpec((depth, span, kv_width), lambda i, place: (0, i, 0))
    return (
        pl.BlockSpec((span, q_all.shape[1]), lambda i, place: (i, 0)),
        [kv_spec] * depth + [sibling],
        pl.BlockSpec((1, groups, GROUP * span, 1), lambda i, place: (i, 0, 0, 0)),
        groups,
    )


def attend(place, q_all, kv_all, span):
    rows = q_all.shape[0]
    q_spec, kv_specs, lse_spec, groups = attend_specs(q_all, kv_all, span)
    cells = rows * groups * GROUP * span * (2 * len(kv_all) - 2)
    return pl.pallas_call(
        attend_kernel,
        grid_spec=pltpu.PrefetchScalarGridSpec(
            num_scalar_prefetch=1,
            grid=(rows // span,),
            in_specs=[q_spec] + kv_specs,
            out_specs=[q_spec, lse_spec],
        ),
        out_shape=(
            jax.ShapeDtypeStruct(q_all.shape, BF),
            jax.ShapeDtypeStruct((rows // span, groups, GROUP * span, 1), F32),
        ),
        compiler_params=pltpu.CompilerParams(vmem_limit_bytes=56 << 20),
        cost_estimate=cost(
            flops=2 * 4 * LANES * cells, transcendentals=cells, bytes_accessed=16 << 20
        ),
        name="attend",
    )(place, q_all, *kv_all)


def attend_back(place, q_all, do_all, lse, kv_all, span):
    rows = q_all.shape[0]
    q_spec, kv_specs, lse_spec, groups = attend_specs(q_all, kv_all, span)
    cells = rows * groups * GROUP * span * (2 * len(kv_all) - 2)
    outs = pl.pallas_call(
        attend_back_kernel,
        grid_spec=pltpu.PrefetchScalarGridSpec(
            num_scalar_prefetch=1,
            grid=(rows // span,),
            in_specs=[q_spec, q_spec, lse_spec] + kv_specs,
            out_specs=[q_spec] + kv_specs,
        ),
        out_shape=[jax.ShapeDtypeStruct(q_all.shape, BF)]
        + [jax.ShapeDtypeStruct(kv.shape, BF) for kv in kv_all],
        compiler_params=pltpu.CompilerParams(vmem_limit_bytes=60 << 20),
        cost_estimate=cost(
            flops=2 * 8 * LANES * cells, transcendentals=cells, bytes_accessed=24 << 20
        ),
        name="attend_back",
    )(place, q_all, do_all, lse, *kv_all)
    return outs[0], outs[1:]


def spread_kernel(place_ref, own_ref, other_ref, out_ref):
    @pl.when(pl.program_id(1) == 0)
    def _():
        out_ref[...] = own_ref[0].astype(F32)

    @pl.when(pl.program_id(1) == 1)
    def _():
        out_ref[...] = other_ref[0].astype(F32)


def spread(own, other, c, axis):
    count, high, wide = own.shape
    shape = {
        0: (high * 2 * count, wide),
        1: (high, wide * 2 * count),
        2: (high * 2, wide * count),
    }[axis]

    def out_place(i, side, place):
        core = (place[0] + side) % 2
        return [(2 * i + core, 0), (0, 2 * i + core), (core, i)][axis]

    return pl.pallas_call(
        spread_kernel,
        grid_spec=pltpu.PrefetchScalarGridSpec(
            num_scalar_prefetch=1,
            grid=(count, 2),
            in_specs=[pl.BlockSpec((1, high, wide), lambda i, side, place: (i, 0, 0))] * 2,
            out_specs=pl.BlockSpec((high, wide), out_place),
        ),
        out_shape=jax.ShapeDtypeStruct(shape, F32),
        compiler_params=pltpu.CompilerParams(vmem_limit_bytes=48 << 20),
        cost_estimate=cost(
            flops=own.size, transcendentals=0, bytes_accessed=12 * own.size
        ),
        name="spread",
    )(c.astype(jnp.int32)[None], own, other)


def spread_half(own, other, c, half, base):
    high, wide = own.shape
    scalars = jnp.stack([c, 1 - c]).astype(jnp.int32)

    def kernel(place_ref, own_ref, other_ref, *refs):
        out_ref = refs[-1]

        @pl.when(pl.program_id(0) == 0)
        def _():
            out_ref[...] = own_ref[...].astype(F32)

        @pl.when(pl.program_id(0) == 1)
        def _():
            out_ref[...] = other_ref[...].astype(F32)

    more = [] if base is None else [base]
    return pl.pallas_call(
        kernel,
        grid_spec=pltpu.PrefetchScalarGridSpec(
            num_scalar_prefetch=1,
            grid=(2,),
            in_specs=[pl.BlockSpec((high, wide), lambda side, place: (0, 0))] * 2
            + [pl.BlockSpec(memory_space=pl.ANY)] * len(more),
            out_specs=pl.BlockSpec((high, wide), lambda side, place: (2 * place[side] + half, 0)),
        ),
        out_shape=jax.ShapeDtypeStruct((4 * high, wide), F32),
        input_output_aliases={3: 0} if more else {},
        compiler_params=pltpu.CompilerParams(vmem_limit_bytes=48 << 20),
        cost_estimate=cost(flops=own.size, transcendentals=0, bytes_accessed=12 * own.size),
        name="spread_half",
    )(scalars, own, other, *more)


def dot(left, right):
    return jnp.dot(left, right, preferred_element_type=F32)


def dot_t(left, right):
    return lax.dot_general(left, right, (((1,), (1,)), ((), ())), preferred_element_type=F32)


def t_dot(left, right):
    return lax.dot_general(left, right, (((0,), (0,)), ((), ())), preferred_element_type=F32)


def exchange(field):
    return lax.all_to_all(field, "fsdp", split_axis=0, concat_axis=0, tiled=True)


def by_chunk(field, f):
    count = field.shape[0]
    return [lax.dynamic_index_in_dim(field, f ^ r, 0, keepdims=False) for r in range(count)]


def by_core(own, other, axis):
    first = lax.axis_index("core") == 0
    return jnp.stack([jnp.where(first, own, other), jnp.where(first, other, own)], axis)


def take(field, index, size, axis):
    return lax.dynamic_slice_in_dim(field, index * size, size, axis)


def body(
    tokens,
    positions,
    gain_attn,
    w_query,
    w_key,
    w_value,
    w_out,
    gain_ffn,
    w_gate,
    w_up,
    w_down,
    grad_out,
):
    seq_count, span, width = tokens.shape
    rows = seq_count * span
    count = lax.axis_size("fsdp")
    depth = lax.axis_size("zed")
    f = lax.axis_index("fsdp")
    z = lax.axis_index("zed")
    c = lax.axis_index("core")
    shard = width // count
    half_shard = shard // 2
    q_width = HEADS * HEAD_DIM // count
    k_width = KV_HEADS * HEAD_DIM // count
    kv_local = KV_HEADS // count
    ff = w_gate.shape[1]
    ff_half = ff // count // 2
    place = jnp.stack([z, c]).astype(jnp.int32)

    x_own = tokens.reshape(rows, width)
    x_list, _ = gather_rel(x_own)
    small = jnp.concatenate(
        [gain_attn.astype(F32), gain_ffn.astype(F32), positions.reshape(rows).astype(F32)]
    ).reshape(-1, LANES)
    small_list = [small] + [xor_send(small, r) for r in range(1, count)]
    gain_rows = shard // LANES

    def by_index(pieces):
        bit = 1
        while bit < count:
            odd = (f // bit) % 2 == 1
            pieces = [jnp.where(odd, pieces[i ^ bit], pieces[i]) for i in range(count)]
            bit *= 2
        return jnp.concatenate(pieces, 0)

    gain_one = by_index([piece[:gain_rows] for piece in small_list]).reshape(1, width)
    gain_two = by_index([piece[gain_rows : 2 * gain_rows] for piece in small_list]).reshape(
        1, width
    )
    places = jnp.concatenate([piece[2 * gain_rows :].reshape(rows) for piece in small_list])
    half_dim = HEAD_DIM // 2
    lane = jnp.arange(LANES, dtype=jnp.int32)
    freqs = jnp.exp((lane % half_dim).astype(F32) * (-2.0 * theta_log / (2 * half_dim)))
    angles = places[:, None] * freqs
    cos_tab = jnp.cos(angles)
    sin_tab = jnp.sin(angles) * jnp.where(lane % HEAD_DIM < half_dim, -1.0, 1.0)

    all_width = q_width + 2 * k_width
    w_own = exchange(pick_heads(place, w_query, w_key, w_value, count))
    w_other = core_swap(w_own)

    w0, x_list, cos_tab, sin_tab, gain_one = lax.optimization_barrier(
        (pick_units(place, w_gate, w_up, count), x_list, cos_tab, sin_tab, gain_one)
    )
    w0 = exchange(w0).reshape(width, ff_half)

    kv_width = 2 * k_width
    h_list, q_list, kv_list = [], [], []
    for r in range(count):
        piece = slice(r * rows, (r + 1) * rows)
        h, q, kv = project(
            place, x_list[r], gain_one, w_own, w_other, cos_tab[piece], sin_tab[piece], kv_width
        )
        h_list.append(h)
        q_list.append(q)
        kv_list.append(kv)
    h_all = jnp.concatenate(h_list, 0)
    q_all = jnp.concatenate(q_list, 0)
    stream = jnp.concatenate(kv_list, 0)
    kv_all = [stream]
    sibling = core_swap(stream)
    for step in range(1, depth):
        stream = z_up(stream)
        if step == 1:
            stream, w0 = lax.optimization_barrier((stream, w0))
        kv_all.append(stream)
    others = core_swap(jnp.stack(kv_all[1:]))
    kv_all = kv_all + [jnp.concatenate([sibling[None], others], 0)]
    w1, _ = lax.optimization_barrier((w0, stream))
    w1 = lax.ppermute(w1, "zed", [(i, i ^ 1) for i in range(depth)])
    cot_own = grad_out.reshape(rows, width)
    cot_abs, _ = lax.optimization_barrier((cot_own, w0))
    cot_abs = lax.all_gather(cot_abs, "fsdp", axis=0, tiled=True)
    attended, lse = attend(place, q_all, kv_all, span)
    w0 = [w0, core_swap(w0)]
    attended, cot_abs, w0 = lax.optimization_barrier((attended, cot_abs, w0))


    def chunk(field, r):
        return field[r * rows : (r + 1) * rows]

    branch = [dot(chunk(attended, r), w_out) for r in range(count)]
    branch = reduce_rel([branch[0]] + [part.astype(BF) for part in branch[1:]])
    cot_all = jnp.concatenate([take(cot_abs, f ^ r, rows, 0) for r in range(count)], 0)
    branch, cot_all = lax.optimization_barrier((branch, cot_all))
    x_float = x_own.astype(F32)
    resid = x_float + branch
    inv_two = lax.rsqrt(jnp.mean(resid * resid, -1, keepdims=True) + norm_eps)
    resid_hat = resid * inv_two
    h2_list, w1 = gather_rel((resid_hat * gain_two).astype(BF), w1)
    h2_all = jnp.concatenate(h2_list, 0)
    w1 = [w1, core_swap(w1)]

    def summed(left, right):
        other = core_swap(t_dot(left, right[1]).astype(BF))
        return (t_dot(left, right[0]) + other.astype(F32)).astype(BF)

    cut = width // 2
    fed = [None, feed(place, h2_all, cot_all, w0[1], w1[1], w_down, 1)]
    h2_late, fed[1] = lax.optimization_barrier((h2_all, fed[1]))
    fed[0] = feed(place, h2_late, cot_all, w0[0], w1[0], w_down, 0)
    hidden, d_gate, d_up = zip(*fed)
    gate0 = summed(h2_all[:, :cut], d_gate)
    gate0, d_gate, d_up = lax.optimization_barrier((gate0, d_gate, d_up))
    middle = count // 2 * rows
    far = unfeed(place, d_gate, d_up, w0, w1, middle, count * rows)
    near = unfeed(place, d_gate, d_up, w0, w1, 0, middle)

    def core_sum(own, other):
        return add_low(own, core_swap(other))

    near, late = lax.optimization_barrier((near, (h2_all, hidden, cot_all)))
    d_h2 = reduce_rel([chunk(part, r) for part in (near, far) for r in range(count // 2)])
    down = lower(place, hidden, w_down)
    line = Line()
    h2_late, hidden_late, cot_late = late
    gate1 = summed(h2_late[:, cut:], d_gate)
    d_h2, down = line.round((d_h2, down), gate0=gate0)
    up_sum = summed(h2_late, d_up)
    up_parts = [up_sum[:cut], up_sum[cut:]]
    down_part = core_sum(*[t_dot(hidden_late[side], cot_late).astype(BF) for side in range(2)])

    d_hat_two = d_h2 * gain_two
    part_gain_two = jnp.sum(d_h2 * resid_hat, 0)
    d_resid = cot_own.astype(F32) + inv_two * (
        d_hat_two - resid_hat * jnp.mean(d_hat_two * resid_hat, -1, keepdims=True)
    )
    d_branch, _ = gather_rel(d_resid.astype(BF))
    d_branch = line.round(d_branch, gate1=gate1)
    d_branch = jnp.concatenate(d_branch, 0)
    d_attended = dot_t(d_branch, w_out).astype(BF)
    dq, dkv_all = attend_back(place, q_all, d_attended, lse, kv_all, span)
    dq, dkv_all, down = line.round((dq, dkv_all, down), up0=up_parts[0])
    d_q = unrotate(dq, cos_tab, sin_tab, rows)
    up_last = up_parts[1]
    tail = None
    from_sibling = core_swap(dkv_all[-1])
    for step in reversed(range(depth)):
        here = dkv_all[step].astype(F32) + from_sibling[step].astype(F32)
        if tail is not None:
            moved = z_down(tail)
            if step == depth - 2:
                moved, up_last = line.hold((moved, up_last))
            here = here + moved.astype(F32)
        tail = here.astype(BF)
    down = reduce_rel([chunk(down, r) for r in range(count)])
    layer_out = (resid + down).astype(BF).reshape(seq_count, span, width)
    tail, layer_out = line.round((tail, layer_out), up1=up_last)
    def row_pair(field):
        field = field.astype(BF).reshape(count, 2, half_shard, -1)
        own = lax.dynamic_index_in_dim(field, c, 1, keepdims=False)
        other = lax.dynamic_index_in_dim(field, 1 - c, 1, keepdims=False)
        return own, other

    g_q = row_pair(t_dot(h_all, d_q))
    d_branch, _ = lax.optimization_barrier((d_branch, d_q))
    g_out = t_dot(attended, d_branch).astype(BF)
    out_half = q_width // 2
    g_out = (take(g_out, c, out_half, 0), take(g_out, 1 - c, out_half, 0))
    g_qo = core_sum(
        *[
            jnp.concatenate([q.reshape(-1, q_width), out.reshape(-1, q_width)], 0)
            for q, out in zip(g_q, g_out)
        ]
    )
    d_kv, d_h1_all = unproject(place, d_q, tail, w_own, w_other, cos_tab, sin_tab)
    d_h1 = reduce_rel([chunk(d_h1_all, r) for r in range(count)])
    g_kv = core_sum(*row_pair(t_dot(h_all, d_kv)))
    d_h1, g_kv = line.round((d_h1, g_kv), qo=g_qo)

    inv_one = lax.rsqrt(jnp.mean(x_float * x_float, -1, keepdims=True) + norm_eps)
    x_hat = x_float * inv_one
    d_hat_one = d_h1 * gain_one
    part_gain_one = jnp.sum(d_h1 * x_hat, 0)
    d_input = d_resid + inv_one * (
        d_hat_one - x_hat * jnp.mean(d_hat_one * x_hat, -1, keepdims=True)
    )
    grad_tokens = d_input.astype(BF).reshape(seq_count, span, width)
    gains = jnp.stack([part_gain_one, part_gain_two], 1)
    gains = jnp.pad(gains, ((0, 0), (0, LANES - 2)))
    gains = reduce_rel(by_chunk(gains.astype(BF).reshape(count, shard, LANES), f))
    gains = gains.astype(BF)
    gains = core_sum(take(gains, c, half_shard, 0), take(gains, 1 - c, half_shard, 0))

    def pair_rows(own):
        return spread(own[None], core_swap(own)[None], c, 0)

    def to_rows(own):
        own = exchange(own.reshape(count, shard, ff_half))
        return spread(own, core_swap(own), c, 1)

    cut = ff_half // 2
    gains = line.round(gains, kv=g_kv, down0=down_part[:cut])

    def whole(name):
        return jnp.concatenate(line.take(name + "0", name + "1"), 0)

    grad_gate = to_rows(whole("gate"))
    grad_gate = line.round(grad_gate, gains=gains, down1=down_part[cut:])
    grad_up = to_rows(whole("up"))
    (g_qo,) = line.take("qo")
    high = count * half_shard
    grad_out_w = pair_rows(g_qo[high:].reshape(out_half, width))
    g_q = exchange(g_qo[:high].reshape(count, half_shard, q_width))
    grad_q = spread(g_q, core_swap(g_q), c, 2)
    grad_up, grad_out_w, grad_q = line.round((grad_up, grad_out_w, grad_q))
    (g_kv,) = line.take("kv")
    g_kv = exchange(g_kv)
    g_kv = by_core(g_kv, core_swap(g_kv), 0).astype(F32)
    g_kv = jnp.transpose(g_kv, (0, 2, 1, 3)).reshape(shard, count * kv_local, 2, HEAD_DIM)
    grad_k = g_kv[:, :, 0].reshape(shard, count * k_width)
    grad_v = g_kv[:, :, 1].reshape(shard, count * k_width)
    (first,) = line.take("down0")
    grad_down = spread_half(first, core_swap(first), c, 0, None)
    grad_k, grad_v, grad_down = line.round((grad_k, grad_v, grad_down))
    (gains,) = line.take("gains")
    gains = by_core(gains, core_swap(gains), 0).astype(F32).reshape(shard, LANES)
    (second,) = line.take("down1")
    grad_down = spread_half(second, core_swap(second), c, 1, grad_down)
    return (
        layer_out,
        grad_tokens,
        gains[:, 0],
        grad_q,
        grad_k,
        grad_v,
        grad_out_w,
        gains[:, 1],
        grad_gate,
        grad_up,
        grad_down,
    )


def solution(mesh):
    fsdp, seq = mesh.devices.shape
    split = Mesh(mesh.devices.reshape(fsdp, seq // 2, 2), ("fsdp", "zed", "core"))
    field = P("fsdp", ("zed", "core"), None)
    vector = P("fsdp")
    matrix = P("fsdp", None)
    return jax.shard_map(
        body,
        mesh=split,
        in_specs=(
            field,
            P("fsdp", ("zed", "core")),
            vector,
            matrix,
            matrix,
            matrix,
            matrix,
            vector,
            matrix,
            matrix,
            matrix,
            field,
        ),
        out_specs=(
            field,
            field,
            vector,
            matrix,
            matrix,
            matrix,
            matrix,
            vector,
            matrix,
            matrix,
            matrix,
        ),
        check_vma=False,
    )
```
